256 devices in a mesh: sec: 32 (over z_hi, y, core), narrow: 8 (over x, z_lo).
Axes of the slice: x: 4, y: 4, z: 8 (z_hi: 4, z_lo: 2; z = z_hi * 2 + z_lo), core: 2. Of those that a mesh axis runs over, the one named last changes fastest.
Arguments:
- tokens: bfloat16 [4096, 2048], P('sec'), may hold values from -8 to 8
- attn_gain: float32 [2048], replicated, may hold values from 0.5 to 1.5
- w_query: bfloat16 [2048, 4096], P(None, 'narrow'), may hold values from -0.125 to 0.125
- w_key: bfloat16 [2048, 512], P(None, 'narrow'), may hold values from -0.125 to 0.125
- w_value: bfloat16 [2048, 512], P(None, 'narrow'), may hold values from -0.125 to 0.125
- query_gain: float32 [128], replicated, may hold values from 0.6 to 6
- key_gain: float32 [128], replicated, may hold values from 0.6 to 6
- w_out: bfloat16 [4096, 2048], P('narrow'), may hold values from -0.09375 to 0.09375
- moe_gain: float32 [2048], replicated, may hold values from 0.5 to 1.5
- expert_ids: int32 [4096, 8], P('sec'), may hold values from 0 to 127, all different within a row; in each aligned block of 16 rows (0 to 15, 16 to 31, ...) at most 2 rows name the same one
- expert_weights: float32 [4096, 8], P('sec'), may hold values from 0.05 to 1
- w_gate: bfloat16 [128, 2048, 768], P('sec', None, 'narrow'), may hold values from -0.125 to 0.125
- w_up: bfloat16 [128, 2048, 768], P('sec', None, 'narrow'), may hold values from -0.125 to 0.125
- w_down: bfloat16 [128, 768, 2048], P('sec', 'narrow'), may hold values from -0.21875 to 0.21875
Outputs:
- layer_out: bfloat16 [4096, 2048], P(('sec', 'narrow'))
The draws below stay inside these ranges and needn't reach their ends.
Inputs may be any that keep to these rules, and one draw needn't show every extreme that they name: `expert_ids`: each row names 8 different experts. In each aligned block of 16 rows no expert is named by more than 2 rows, a bound that some block reaches.
All inputs are finite; a program needn't handle non-finite values.
Results may differ from the reference program's by a relative error of at most 0.009.
Values may be sent and summed in bfloat16 or wider, within the bound.
No kernel may reach another device: no remote copies, remote signals or barrier semaphores. Data moves between devices by JAX's collectives and lax.ppermute only.
A program may use at most 128 MiB of HBM per device.

```python
import math
import jax
import jax.numpy as jnp
import numpy as np
from jax import lax

D = 2048
HEADS = 32
KV_HEADS = 4
HEAD = 128
FE = 768
TOPK = 8
EXPERTS = 128
TOKENS = 4096
ROWS_N = 16
CAP = 2
N_NARROW = 8


def draw_tokens(key, part):
    noise_key = jax.random.fold_in(key, 0)
    noise = jax.random.normal(noise_key, (TOKENS, D), jnp.float32)
    drawn = noise
    return jnp.clip(drawn, -8.0, 8.0).astype(jnp.bfloat16)


def gain_values(key, salt):
    inner = jax.random.fold_in(key, salt)
    return jax.random.uniform(inner, (HEAD,), jnp.float32, 0.6, 1.6)


def draw_query_gain(key, part):
    return gain_values(key, 11)


def draw_key_gain(key, part):
    return gain_values(key, 23)


def shard_levels(stream_key, shape, shards, smallest, largest):
    level = 1.0
    for axis_at, shards_of in shards:
        steps = jax.random.uniform(jax.random.fold_in(jax.random.fold_in(stream_key, 6), axis_at), (shards_of,), jnp.float32, smallest / len(shards), largest / len(shards))
        level = level * jnp.repeat(jnp.exp(steps), shape[axis_at] // shards_of).reshape((-1,) + (1,) * (len(shape) - 1 - axis_at))
    return level


def deal_out(rng, own, number, rows, amount, top, limit, lean):
    ranking = jax.random.permutation(rng, amount)
    heavy_load, ordinary = portions_of(amount, rows * top, limit, lean, True), portions_of(amount, rows * top, limit, lean, False)
    places = jnp.arange(amount)

    def named(tallies, offset_by):
        used = int((tallies > 0).sum())
        fixed = max(1, used // 4)
        moved = fixed + (places - fixed + offset_by * (used - fixed)) % max(1, amount - fixed)
        return jnp.zeros((amount,), jnp.int32).at[ranking[jnp.where(places < fixed, places, moved)]].set(jnp.asarray(tallies, jnp.int32))

    tallies = jnp.where(number % 4 == 0, named(heavy_load, number // 4), named(ordinary, number - number // 4 - 1))
    mixed = jax.random.permutation(jax.random.fold_in(own, 3), amount)
    donor, receiver = mixed[0:amount // 2 * 2:2], mixed[1:amount // 2 * 2:2]
    margin = jnp.minimum(tallies[donor] - 1, limit - tallies[receiver]) // 2
    margin = jnp.where((donor == ranking[0]) | (receiver == ranking[0]) | (tallies[receiver] == 0), 0, jnp.maximum(margin, 0))
    moved = jax.random.randint(jax.random.fold_in(own, 4), (amount // 2,), 0, 1 << 20) % (margin + 1)
    tallies = tallies.at[donor].add(-moved).at[receiver].add(moved)
    items = jnp.searchsorted(jnp.cumsum(tallies), jnp.arange(rows * top), side="right").astype(jnp.int32)
    listing = items.reshape(top, rows).T
    listing = listing[jax.random.permutation(jax.random.fold_in(own, 1), rows)]
    offset_by = jax.random.randint(jax.random.fold_in(own, 2), (rows, 1), 0, top)
    return jnp.take_along_axis(listing, (jnp.arange(top)[None, :] + offset_by) % top, axis=1)


def portions_of(number_of, total, reach, slope, full):
    portions = [(1 << 20) // math.isqrt(grade ** slope) + 1 for grade in range(1, number_of + 1)]
    largest = reach if full else min(reach, max(-(-total // number_of), total * portions[0] // sum(portions)))
    least = 1 if total - largest >= number_of - 1 else 0
    counts, rest = [largest] + [least] * (number_of - 1), total - largest - least * (number_of - 1)
    while rest > 0:
        movable = [i for i in range(1, number_of) if counts[i] < largest] or [i for i in range(1, number_of) if counts[i] < reach]
        mass, left = sum([portions[i] for i in movable]), rest
        for i in movable:
            extra = min(reach - counts[i], max(1, left * portions[i] // mass), rest)
            counts[i] = counts[i] + extra
            rest = rest - extra
    return np.array(counts)


def normal_values(rng, extent, spread, most, cuts=(), held_as=jnp.bfloat16):
    values = jax.random.normal(rng, extent, jnp.float32) * spread
    if len(cuts) > 0:
        values = shard_levels(rng, extent, cuts, -0.22, 0.18) * values
    return jnp.clip(values, min=-most, max=most).astype(held_as)


def setup_inputs(seed: int = 0) -> dict:
    arg_keys = jax.random.split(jax.random.key(seed), 15)
    tokens = draw_tokens(jax.random.fold_in(arg_keys[14], 71), 0)
    attn_gain = jnp.clip(1.0 + 0.1 * jax.random.normal(arg_keys[1], (D,), jnp.float32), 0.5, 1.5)
    w_query = normal_values(arg_keys[2], (D, HEADS * HEAD), D ** -0.5, 0.125, ((1, 8),))
    w_key = normal_values(arg_keys[3], (D, KV_HEADS * HEAD), D ** -0.5, 0.125, ((1, 8),))
    w_value = normal_values(arg_keys[4], (D, KV_HEADS * HEAD), D ** -0.5, 0.125, ((1, 8),))
    query_gain = draw_query_gain(jax.random.fold_in(arg_keys[14], 71), 0)
    key_gain = draw_key_gain(jax.random.fold_in(arg_keys[14], 71), 0)
    w_out = normal_values(arg_keys[7], (HEADS * HEAD, D), (HEADS * HEAD) ** -0.5, 0.09375, ((0, 8),))
    moe_gain = jnp.clip(1.0 + 0.1 * jax.random.normal(arg_keys[8], (D,), jnp.float32), 0.5, 1.5)
    expert_ids_keys = jax.random.split(jax.random.fold_in(arg_keys[9], 1), TOKENS // ROWS_N)
    expert_ids_turns = jax.random.permutation(jax.random.fold_in(arg_keys[9], 3), TOKENS // ROWS_N)
    expert_ids = jax.vmap(lambda own, number: deal_out(jax.random.fold_in(arg_keys[9], 2), own, number, ROWS_N, EXPERTS, TOPK, CAP, 2))(expert_ids_keys, expert_ids_turns).reshape((TOKENS, TOPK))
    expert_weights = jnp.clip(jnp.exp(math.log(1.0) - 2.9957323 * jax.random.uniform(arg_keys[10], (TOKENS, TOPK), jnp.float32) ** shard_levels(arg_keys[10], (TOKENS, TOPK), ((0, 32),), -0.2, 0.2)), 0.05, 1.0)
    w_gate = normal_values(arg_keys[11], (EXPERTS, D, FE), D ** -0.5, 0.125, ((0, 32), (2, 8)))
    w_up = normal_values(arg_keys[12], (EXPERTS, D, FE), D ** -0.5, 0.125, ((0, 32), (2, 8)))
    w_down = normal_values(arg_keys[13], (EXPERTS, FE, D), FE ** -0.5, 0.21875, ((0, 32), (1, 8)))
    return {"tokens": tokens, "attn_gain": attn_gain, "w_query": w_query, "w_key": w_key, "w_value": w_value, "query_gain": query_gain, "key_gain": key_gain, "w_out": w_out, "moe_gain": moe_gain, "expert_ids": expert_ids, "expert_weights": expert_weights, "w_gate": w_gate, "w_up": w_up, "w_down": w_down}


norm_eps = 1e-06

def rms_norm(inputs, gain):
    widened = inputs.astype(jnp.float32)
    return widened * lax.rsqrt(lax.optimization_barrier(jnp.mean(widened * widened, axis=-1, keepdims=True)) + norm_eps) * gain

def rotate(inputs, positions):
    half_size = inputs.shape[-1] // 2
    inverse = jnp.exp(-jnp.log(1000000.0) * jnp.arange(half_size, dtype=jnp.float32) * 2.0 / inputs.shape[-1])
    angles = positions.astype(jnp.float32)[:, None] * inverse[None, :]
    cosine = jnp.cos(angles)[:, None, :]
    sine = jnp.sin(angles)[:, None, :]
    leading = inputs[..., :half_size]
    trailing = inputs[..., half_size:]
    return jnp.concatenate([leading * cosine - trailing * sine, trailing * cosine + leading * sine], axis=-1)

def reference(tokens, attn_gain, w_query, w_key, w_value, query_gain, key_gain, w_out, moe_gain, expert_ids, expert_weights, w_gate, w_up, w_down):
    length = tokens.shape[0]
    positions = jnp.arange(length, dtype=jnp.int32)
    normed = rms_norm(tokens, attn_gain).astype(jnp.bfloat16)
    query = jnp.dot(normed, w_query, preferred_element_type=jnp.float32).reshape(length, HEADS, HEAD)
    query = rotate(rms_norm(query, query_gain), positions).astype(jnp.bfloat16)
    keys = jnp.dot(normed, w_key, preferred_element_type=jnp.float32).reshape(length, HEAD, KV_HEADS)
    keys = jnp.transpose(keys, (0, 2, 1))
    keys = rotate(rms_norm(keys, key_gain), positions).astype(jnp.bfloat16)
    values = jnp.dot(normed, w_value, preferred_element_type=jnp.float32).astype(jnp.bfloat16).reshape(length, HEAD, KV_HEADS)
    values = jnp.transpose(values, (0, 2, 1))
    group_size = HEADS // KV_HEADS
    scale = 1.0 / math.sqrt(HEAD)
    allowed = positions[None, :] <= positions[:, None]
    key_heads = jnp.transpose(keys, (1, 0, 2))
    value_heads = jnp.transpose(values, (1, 0, 2))

    def one_head(inputs):
        query_head, number = inputs
        key_head = lax.dynamic_index_in_dim(key_heads, number // group_size, 0, keepdims=False)
        value_head = lax.dynamic_index_in_dim(value_heads, number // group_size, 0, keepdims=False)
        scores = jnp.dot(query_head, key_head.T, preferred_element_type=jnp.float32) * scale
        scores = jnp.where(allowed, scores, -1e+30)
        peak = lax.optimization_barrier(jnp.max(scores, axis=-1, keepdims=True))
        probs = jnp.where(allowed, jnp.exp(scores - peak), 0.0)
        summed = jnp.dot(probs.astype(jnp.bfloat16), value_head, preferred_element_type=jnp.float32)
        return (summed / lax.optimization_barrier(jnp.sum(probs, axis=-1, keepdims=True))).astype(jnp.bfloat16)
    attended = lax.map(one_head, (jnp.transpose(query, (1, 0, 2)), jnp.arange(HEADS, dtype=jnp.int32)))
    attended = jnp.transpose(attended, (1, 0, 2)).reshape(length, HEADS * HEAD)
    carried = (tokens.astype(jnp.float32) + jnp.dot(attended, w_out, preferred_element_type=jnp.float32)).astype(jnp.bfloat16)
    moe_in = rms_norm(carried, moe_gain).astype(jnp.bfloat16)
    gates = expert_weights / lax.optimization_barrier(jnp.sum(expert_weights, axis=-1, keepdims=True))
    blocks = length // ROWS_N
    flat_ids = expert_ids.reshape(blocks, ROWS_N * TOPK)
    onehot = (flat_ids[:, :, None] == jnp.arange(EXPERTS, dtype=jnp.int32)[None, None, :]).astype(jnp.int32)
    earlier = jnp.cumsum(onehot, axis=1) - onehot
    slots = lax.optimization_barrier(jnp.sum(earlier * onehot, axis=-1))
    per_expert = blocks * CAP
    places = flat_ids * per_expert + jnp.arange(blocks, dtype=jnp.int32)[:, None] * CAP + slots
    sources = jnp.arange(length * TOPK, dtype=jnp.int32) // TOPK
    table = jnp.full((EXPERTS * per_expert,), length, jnp.int32).at[places.reshape(-1)].set(sources)
    padded = jnp.concatenate([moe_in, jnp.zeros((1, D), jnp.bfloat16)], axis=0)
    routed = padded[table].reshape(EXPERTS, per_expert, D)
    group_width = FE // N_NARROW

    def one_expert(inputs):
        rows_in, gate_matrix, up_matrix, down_matrix = inputs
        gate_value = jnp.dot(rows_in, gate_matrix, preferred_element_type=jnp.float32)
        up_value = jnp.dot(rows_in, up_matrix, preferred_element_type=jnp.float32)
        active = (jax.nn.silu(gate_value) * up_value).astype(jnp.bfloat16)
        total = jnp.zeros((per_expert, D), jnp.float32)
        for group_index in range(N_NARROW):
            lower = group_index * group_width
            partial_term = jnp.dot(active[:, lower:lower + group_width], down_matrix[lower:lower + group_width], preferred_element_type=jnp.float32)
            rounded = lax.optimization_barrier(partial_term.astype(jnp.bfloat16))
            total = total + rounded.astype(jnp.float32)
        return total.astype(jnp.bfloat16)
    outputs = lax.map(one_expert, (routed, w_gate, w_up, w_down)).reshape(EXPERTS * per_expert, D)
    picked = outputs[places.reshape(-1)].reshape(length, TOPK, D)
    mixture = lax.optimization_barrier(jnp.sum(gates[:, :, None] * picked.astype(jnp.float32), axis=1))
    return (carried.astype(jnp.float32) + mixture).astype(jnp.bfloat16)
```

```python
import functools
import math

import jax
import jax.numpy as jnp
from jax import lax
from jax.experimental import pallas as pl
from jax.experimental.pallas import tpu as pltpu
from jax.sharding import Mesh
from jax.sharding import PartitionSpec as P

D = 2048
HEADS = 32
KV_HEADS = 4
HEAD = 128
TOPK = 8
CAP = 2
ZH, Y, C, X, ZL = 4, 4, 2, 4, 2
SEC = ("zh", "y", "c")
NARROW = ("x", "zl")
PLANE = ("y", "x", "zl")

norm_eps = 1e-06
BF = jnp.bfloat16
F32 = jnp.float32


def rms_norm(inputs, gain):
    widened = inputs.astype(F32)
    return (
        widened * lax.rsqrt(jnp.mean(widened * widened, axis=-1, keepdims=True) + norm_eps) * gain
    )


def angles_of(positions):
    half = HEAD // 2
    inverse = jnp.exp(-jnp.log(1000000.0) * jnp.arange(half, dtype=F32) * 2.0 / HEAD)
    angles = positions.astype(F32)[:, None] * inverse[None, :]
    return jnp.cos(angles), jnp.sin(angles)


def attention_kernel(where_ref, q_ref, own_ref, other_ref, w_out_ref, out_ref, acc, peak, total, attended):
    rows = q_ref.shape[0]
    heads = q_ref.shape[1] // HEAD
    pair_here = where_ref[0]
    core = where_ref[1]
    factor = math.log2(math.e) / math.sqrt(HEAD)
    acc[...] = jnp.zeros_like(acc)
    total[...] = jnp.zeros_like(total)
    peak[...] = jnp.full_like(peak, -1e30)

    def step(pair, masks):
        zh = pair // Y
        y = pair % Y
        own_k, own_v = own_ref[y, zh, 0], own_ref[y, zh, 1]
        other_k, other_v = other_ref[y, zh, 0], other_ref[y, zh, 1]
        for h in range(heads):
            q = q_ref[:, h * HEAD : (h + 1) * HEAD]
            s0 = jnp.dot(q, own_k, preferred_element_type=F32) * factor
            s1 = jnp.dot(q, other_k, preferred_element_type=F32) * factor
            if masks is not None:
                s0 = jnp.where(masks[0], s0, -1e30)
                s1 = jnp.where(masks[1], s1, -1e30)
            old = peak[h]
            new = jnp.maximum(old, jnp.max(jnp.maximum(s0, s1), axis=-1, keepdims=True))
            p0 = jnp.exp2(s0 - new)
            p1 = jnp.exp2(s1 - new)
            if masks is not None:
                p0 = jnp.where(masks[0], p0, 0.0)
                p1 = jnp.where(masks[1], p1, 0.0)
            scale = jnp.exp2(old - new)
            total[h] = total[h] * scale + p0 + p1
            acc[h] = (
                acc[h] * scale
                + jnp.dot(p0.astype(BF), own_v, preferred_element_type=F32)
                + jnp.dot(p1.astype(BF), other_v, preferred_element_type=F32)
            )
            peak[h] = new

    @pl.loop(0, pair_here)
    def _(pair):
        step(pair, None)

    row = lax.broadcasted_iota(jnp.int32, (rows, HEAD), 0)
    column = lax.broadcasted_iota(jnp.int32, (rows, HEAD), 1)
    step(pair_here, (column <= row, column < core * HEAD))
    for h in range(heads):
        attended[:, h * HEAD : (h + 1) * HEAD] = (
            acc[h] / jnp.sum(total[h], axis=-1, keepdims=True)
        ).astype(BF)
    width = 512
    for at in range(0, D, width):
        out_ref[:, at : at + width] = jnp.dot(
            attended[...], w_out_ref[:, at : at + width], preferred_element_type=F32
        ).astype(BF)


def attention(where, query, own, other, w_out):
    rows = query.shape[0]
    heads = query.shape[1] // HEAD
    vmem = pl.BlockSpec(memory_space=pltpu.VMEM)
    return pl.pallas_call(
        attention_kernel,
        out_shape=jax.ShapeDtypeStruct((rows, D), BF),
        in_specs=[pl.BlockSpec(memory_space=pltpu.SMEM), vmem, vmem, vmem, vmem],
        out_specs=vmem,
        scratch_shapes=[
            pltpu.VMEM((heads, rows, HEAD), F32),
            pltpu.VMEM((heads, rows, 1), F32),
            pltpu.VMEM((heads, rows, HEAD), F32),
            pltpu.VMEM((rows, heads * HEAD), BF),
        ],
        cost_estimate=pl.CostEstimate(
            flops=1400000000, bytes_accessed=5000000, transcendentals=2000000
        ),
        name="attend",
    )(where, query, own, other, w_out)


def expert_kernel(rows_ref, *refs):
    pieces = refs[:8]
    out_ref, first, down, active, sems = refs[8:]
    width = down.shape[0] // 8

    def first_copy(i):
        return pltpu.make_async_copy(pieces[i].at[pl.ds(0, 2 * width)], first.at[i], sems.at[0, i])

    def down_copy(i):
        return pltpu.make_async_copy(
            pieces[i].at[pl.ds(2 * width, width)], down.at[pl.ds(i * width, width)], sems.at[1, i]
        )

    for i in range(8):
        first_copy(i).start()
    for i in range(8):
        down_copy(i).start()
    rows = rows_ref[...]
    for i in range(8):
        first_copy(i).wait()
        both = lax.dot_general(
            first[i], rows, (((1,), (1,)), ((), ())), preferred_element_type=F32
        )
        gate, up = both[:width], both[width:]
        active[i * width : (i + 1) * width, :] = (gate / (1.0 + jnp.exp(-gate)) * up).astype(BF)
    for i in range(8):
        down_copy(i).wait()
    span = 512
    for at in range(0, D, span):
        out_ref[:, at : at + span] = lax.dot_general(
            active[...],
            down[:, at : at + span],
            (((0,), (0,)), ((), ())),
            preferred_element_type=F32,
        ).astype(BF)


def expert(rows, pieces):
    count = rows.shape[0]
    width = pieces[0].shape[0] // 3
    vmem = pl.BlockSpec(memory_space=pltpu.VMEM)
    hbm = pl.BlockSpec(memory_space=pl.ANY)
    return pl.pallas_call(
        expert_kernel,
        out_shape=jax.ShapeDtypeStruct((count, D), BF),
        in_specs=[vmem] + [hbm] * 8,
        out_specs=vmem,
        scratch_shapes=[
            pltpu.VMEM((8, 2 * width, D), BF),
            pltpu.VMEM((8 * width, D), BF),
            pltpu.VMEM((8 * width, count), BF),
            pltpu.SemaphoreType.DMA((2, 8)),
        ],
        cost_estimate=pl.CostEstimate(
            flops=2400000000, bytes_accessed=11500000, transcendentals=200000
        ),
        name="expert",
    )(rows, *pieces)


def spread(piece, axes, members):
    copies = jnp.broadcast_to(piece[None], (members, *piece.shape))
    return lax.all_to_all(copies, axes, 0, 0, tiled=True)


def turned(axis_size, by):
    return [(i, (i + by) % axis_size) for i in range(axis_size)]


def weight_pieces(w_gate, w_up, w_down, x):
    gate_t = jnp.swapaxes(w_gate, 1, 2)
    up_t = jnp.swapaxes(w_up, 1, 2)
    own = []
    for k in range(X):
        number = (x + k) % X
        piece = jnp.concatenate(
            [lax.dynamic_index_in_dim(w, number, 0, keepdims=False) for w in (gate_t, up_t, w_down)],
            axis=0,
        )
        pairs = []
        for c in range(C):
            for xs in range(X):
                for zl in range(ZL):
                    source = (c * X + xs) * ZL + zl
                    target = (zl * X + (xs + k) % X) * ZL + c
                    pairs.append((source, target))
        own.append(lax.ppermute(piece, ("c", "x", "zl"), pairs))
    other = [lax.ppermute(piece, "c", [(0, 1), (1, 0)]) for piece in own]
    return own + other


def on_device(
    tokens,
    attn_gain,
    w_query,
    w_key,
    w_value,
    query_gain,
    key_gain,
    w_out,
    moe_gain,
    expert_ids,
    expert_weights,
    w_gate,
    w_up,
    w_down,
):
    zh, y, c = lax.axis_index("zh"), lax.axis_index("y"), lax.axis_index("c")
    x, zl = lax.axis_index("x"), lax.axis_index("zl")
    sec = (zh * Y + y) * C + c
    narrow = x * ZL + zl
    local_rows = tokens.shape[0]
    share = local_rows // (X * ZL)
    positions = sec * local_rows + jnp.arange(local_rows, dtype=jnp.int32)
    cosine, sine = angles_of(positions)
    half = HEAD // 2

    pieces = weight_pieces(w_gate, w_up, w_down, x)

    normed = rms_norm(tokens, attn_gain).astype(BF)

    def columns(w):
        turned_w = lax.dot_general(
            w, normed, (((0,), (1,)), ((), ())), preferred_element_type=F32
        )
        return jnp.swapaxes(turned_w.reshape(-1, KV_HEADS, local_rows), 0, 1)

    both = jnp.stack([columns(w_key), columns(w_value)], axis=1)
    both = both.reshape(X * ZL, -1, local_rows)
    one = lax.all_to_all(both, NARROW, 0, 0, tiled=True).reshape(HEAD, local_rows)
    key_t = one * lax.rsqrt(jnp.mean(one * one, axis=0, keepdims=True) + norm_eps)
    key_t = key_t * key_gain[:, None]
    cos_t, sin_t = cosine.T, sine.T
    lead, trail = key_t[:half], key_t[half:]
    key_t = jnp.concatenate(
        [lead * cos_t - trail * sin_t, trail * cos_t + lead * sin_t], axis=0
    ).astype(BF)
    piece = jnp.where(zl == 0, key_t, one.T.astype(BF))
    ring = spread(piece, ("zh", "zl"), ZH * ZL)
    own = spread(ring, "y", Y)
    own = own.reshape(Y, ZH, ZL, HEAD, HEAD)
    other = lax.ppermute(own, "c", [(0, 1), (1, 0)])

    query = jnp.dot(normed, w_query, preferred_element_type=F32).reshape(local_rows, -1, HEAD)
    query = rms_norm(query, query_gain)
    lead, trail = query[..., :half], query[..., half:]
    cos_q, sin_q = cosine[:, None, :], sine[:, None, :]
    query = jnp.concatenate(
        [lead * cos_q - trail * sin_q, trail * cos_q + lead * sin_q], axis=-1
    ).astype(BF)
    query = query.reshape(local_rows, -1)

    where = jnp.stack([zh * Y + y, c]).astype(jnp.int32)
    partial = attention(where, query, own, other, w_out)
    blocks = lax.all_to_all(
        partial.reshape(X * ZL, share, D), NARROW, 0, 0, tiled=True
    )
    mixed = jnp.sum(blocks.astype(F32), axis=0)
    own_tokens = lax.dynamic_slice_in_dim(tokens, narrow * share, share, 0)
    carried = (own_tokens.astype(F32) + mixed).astype(BF)
    moe_in = rms_norm(carried, moe_gain).astype(BF)

    ids = lax.dynamic_slice_in_dim(expert_ids, narrow * share, share, 0)
    weights = lax.dynamic_slice_in_dim(expert_weights, narrow * share, share, 0)
    gates = weights / jnp.sum(weights, axis=-1, keepdims=True)
    gates_high = gates.astype(BF)
    gates_low = (gates - gates_high.astype(F32)).astype(BF)
    tail = jnp.concatenate(
        [
            ids.astype(BF),
            gates_high,
            gates_low,
            jnp.zeros((share, 128 - 3 * TOPK), BF),
        ],
        axis=1,
    )
    packet = jnp.concatenate([moe_in, tail], axis=1)
    packets = jnp.concatenate(
        [packet] + [lax.ppermute(packet, "zh", turned(ZH, k)) for k in range(1, ZH)], axis=0
    )
    rows = packets[:, :D]
    routes = packets[:, D:].astype(F32)
    ids_f = routes[:, :TOPK]
    gates_all = routes[:, TOPK : 2 * TOPK] + routes[:, 2 * TOPK : 3 * TOPK]
    chips = jnp.arange(Y * X * ZL, dtype=jnp.int32)
    expert_of = (
        zh * (Y * X * ZL) + chips // (X * ZL) * (X * ZL) + chips % ZL * X + chips // ZL % X
    ).astype(F32)
    hits = ids_f[:, :, None] == expert_of[None, None, :]
    named = jnp.any(hits, axis=1).reshape(ZH, share, -1)
    gate_of = jnp.sum(jnp.where(hits, gates_all[:, :, None], 0.0), axis=1).reshape(ZH, share, -1)
    named_f = named.astype(F32)
    earlier = jnp.cumsum(named_f, axis=1) - named_f
    slot = jnp.arange(CAP, dtype=F32)
    chosen = named[..., None] & (earlier[..., None] == slot)
    same = jnp.eye(ZH, dtype=jnp.bool_)
    table = chosen[:, :, :, None, :] & same[:, None, None, :, None]
    table = table.reshape(ZH * share, -1)
    shared_gate = jnp.broadcast_to(
        gate_of[:, :, :, None, None], (ZH, share, Y * X * ZL, ZH, CAP)
    ).reshape(ZH * share, -1)
    outgoing = lax.dot_general(
        table.astype(BF), rows, (((0,), (0,)), ((), ())), preferred_element_type=F32
    ).astype(BF)
    arrived = lax.all_to_all(
        outgoing.reshape(Y * X * ZL, ZH * CAP, D), PLANE, 0, 0, tiled=True
    ).reshape(-1, D)
    answers = expert(arrived, pieces)
    returned = lax.all_to_all(
        answers.reshape(Y * X * ZL, ZH * CAP, D), PLANE, 0, 0, tiled=True
    ).reshape(-1, D)
    mixing = jnp.where(table, shared_gate, 0.0)
    mixing_high = mixing.astype(BF)
    mixing_low = (mixing - mixing_high.astype(F32)).astype(BF)
    sums = jnp.dot(mixing_high, returned, preferred_element_type=F32) + jnp.dot(
        mixing_low, returned, preferred_element_type=F32
    )
    sums = sums.reshape(ZH, share, D)
    result = carried.astype(F32) + sums[0]
    for k in range(1, ZH):
        back = lax.ppermute(sums[k].astype(BF), "zh", turned(ZH, -k))
        result = result + back.astype(F32)
    return result.astype(BF)


def solution(mesh):
    split = Mesh(mesh.devices.reshape(ZH, Y, C, X, ZL), ("zh", "y", "c", "x", "zl"))
    in_specs = (
        P(SEC, None),
        P(),
        P(None, NARROW),
        P(None, NARROW),
        P(None, NARROW),
        P(),
        P(),
        P(NARROW, None),
        P(),
        P(SEC, None),
        P(SEC, None),
        P(SEC, None, NARROW),
        P(SEC, None, NARROW),
        P(SEC, NARROW, None),
    )
    out_specs = P(SEC + NARROW, None)
    return jax.shard_map(
        on_device, mesh=split, in_specs=in_specs, out_specs=out_specs, check_vma=False
    )
```

```python
import math

import jax
import jax.numpy as jnp
from jax import lax
from jax.experimental import pallas as pl
from jax.experimental.pallas import tpu as pltpu
from jax.sharding import Mesh
from jax.sharding import PartitionSpec as P


D = 2048
KV_HEADS = 4
HEAD = 128
TOPK = 8
CAP = 2
ZH, Y, C, X, ZL = 4, 4, 2, 4, 2
SEC = ("zh", "y", "c")
NARROW = ("x", "zl")
PLANE = ("y", "x", "zl")

norm_eps = 1e-06
ATTEND_VMEM = 16 * 1024 * 1024
EXPERT_VMEM = 24 * 1024 * 1024
BF = jnp.bfloat16
F32 = jnp.float32


def rms_norm(inputs, gain):
    widened = inputs.astype(F32)
    return (
        widened * lax.rsqrt(jnp.mean(widened * widened, axis=-1, keepdims=True) + norm_eps) * gain
    )


def angles_of(positions):
    half = HEAD // 2
    inverse = jnp.exp(-jnp.log(1000000.0) * jnp.arange(half, dtype=F32) * 2.0 / HEAD)
    angles = positions.astype(F32)[:, None] * inverse[None, :]
    return jnp.cos(angles), jnp.sin(angles)


def attention_kernel(where_ref, q_ref, own_ref, other_ref, w_out_ref, out_ref, q_all, acc, peak, total, attended):
    rows = q_ref.shape[0]
    heads = q_ref.shape[1] // HEAD
    pair_here = where_ref[0]
    core = where_ref[1]
    factor = math.log2(math.e) / math.sqrt(HEAD)
    for h in range(heads):
        q_all[h * rows : (h + 1) * rows, :] = q_ref[:, h * HEAD : (h + 1) * HEAD]
    acc[...] = jnp.zeros_like(acc)
    total[...] = jnp.zeros_like(total)
    peak[...] = jnp.full_like(peak, -1e30)

    def step(group, last):
        zh = group // 2
        y = group % 2 * 2
        sources = ((own_ref, y), (other_ref, y), (own_ref, y + 1), (other_ref, y + 1))
        keys = jnp.concatenate([ref[at, zh, 0] for ref, at in sources], axis=1)
        values = jnp.concatenate([ref[at, zh, 1] for ref, at in sources], axis=0)
        s = jnp.dot(q_all[...], keys, preferred_element_type=F32)
        if last:
            row = lax.broadcasted_iota(jnp.int32, s.shape, 0) % rows
            column = lax.broadcasted_iota(jnp.int32, s.shape, 1)
            piece = column // HEAD
            section = 4 * group + piece // 2 * 2 + jnp.where(piece % 2 == 0, core, 1 - core)
            allowed = section * HEAD + column % HEAD <= (2 * pair_here + core) * rows + row
            s = jnp.where(allowed, s, -1e30)
        parts = [s[:, i * HEAD : (i + 1) * HEAD] for i in range(4)]
        highest = jnp.maximum(jnp.maximum(parts[0], parts[1]), jnp.maximum(parts[2], parts[3]))
        old = peak[...]
        new = jnp.maximum(old, jnp.max(highest, axis=-1, keepdims=True))
        p = jnp.exp2((s - new) * factor)
        if last:
            p = jnp.where(allowed, p, 0.0)
        parts = [p[:, i * HEAD : (i + 1) * HEAD] for i in range(4)]
        scale = jnp.exp2((old - new) * factor)
        total[...] = total[...] * scale + ((parts[0] + parts[1]) + (parts[2] + parts[3]))
        acc[...] = acc[...] * scale + jnp.dot(p.astype(BF), values, preferred_element_type=F32)
        peak[...] = new

    @pl.loop(0, pair_here // 2)
    def _(group):
        step(group, False)

    step(pair_here // 2, True)
    summed = jnp.sum(total[...], axis=-1, keepdims=True)
    for h in range(heads):
        part = slice(h * rows, (h + 1) * rows)
        attended[:, h * HEAD : (h + 1) * HEAD] = (acc[part, :] / summed[part]).astype(BF)
    width = 512
    for at in range(0, D, width):
        out_ref[:, at : at + width] = jnp.dot(
            attended[...], w_out_ref[:, at : at + width], preferred_element_type=F32
        ).astype(BF)


def attention(where, query, own, other, w_out):
    rows = query.shape[0]
    heads = query.shape[1] // HEAD
    vmem = pl.BlockSpec(memory_space=pltpu.VMEM)
    return pl.pallas_call(
        attention_kernel,
        out_shape=jax.ShapeDtypeStruct((rows, D), BF),
        in_specs=[pl.BlockSpec(memory_space=pltpu.SMEM), vmem, vmem, vmem, vmem],
        out_specs=vmem,
        scratch_shapes=[
            pltpu.VMEM((heads * rows, HEAD), BF),
            pltpu.VMEM((heads * rows, HEAD), F32),
            pltpu.VMEM((heads * rows, 1), F32),
            pltpu.VMEM((heads * rows, HEAD), F32),
            pltpu.VMEM((rows, heads * HEAD), BF),
        ],
        compiler_params=pltpu.CompilerParams(vmem_limit_bytes=ATTEND_VMEM),
        cost_estimate=pl.CostEstimate(
            flops=1400000000, bytes_accessed=5000000, transcendentals=2000000
        ),
        name="attend",
    )(where, query, own, other, w_out)


def expert_kernel(rows_ref, *refs):
    pieces = refs[:8]
    out_ref, weights, active, sems = refs[8:]
    width = pieces[0].shape[0] // 3

    def copy(part, i):
        return pltpu.make_async_copy(
            pieces[i].at[pl.ds(part * width, width)],
            weights.at[part, pl.ds(i * width, width)],
            sems.at[part, i],
        )

    for half in range(2):
        for part in range(2):
            for i in range(4):
                copy(part, 4 * half + i).start()
    for i in range(8):
        copy(2, i).start()
    rows = rows_ref[...]
    for half in range(2):
        for part in range(2):
            for i in range(4):
                copy(part, 4 * half + i).wait()
        span = slice(4 * half * width, 4 * (half + 1) * width)
        gate = lax.dot_general(
            weights[0, span], rows, (((1,), (1,)), ((), ())), preferred_element_type=F32
        )
        up = lax.dot_general(
            weights[1, span], rows, (((1,), (1,)), ((), ())), preferred_element_type=F32
        )
        active[span, :] = (gate / (1.0 + jnp.exp(-gate)) * up).astype(BF)
    for i in range(8):
        copy(2, i).wait()
    acts = active[...].T
    span = 512
    for at in range(0, D, span):
        out_ref[:, at : at + span] = jnp.dot(
            acts, weights[2, :, at : at + span], preferred_element_type=F32
        ).astype(BF)


def expert(rows, pieces):
    count = rows.shape[0]
    width = pieces[0].shape[0] // 3
    vmem = pl.BlockSpec(memory_space=pltpu.VMEM)
    hbm = pl.BlockSpec(memory_space=pl.ANY)
    return pl.pallas_call(
        expert_kernel,
        out_shape=jax.ShapeDtypeStruct((count, D), BF),
        in_specs=[vmem] + [hbm] * 8,
        out_specs=vmem,
        scratch_shapes=[
            pltpu.VMEM((3, 8 * width, D), BF),
            pltpu.VMEM((8 * width, count), BF),
            pltpu.SemaphoreType.DMA((3, 8)),
        ],
        compiler_params=pltpu.CompilerParams(vmem_limit_bytes=EXPERT_VMEM),
        cost_estimate=pl.CostEstimate(
            flops=2400000000, bytes_accessed=11500000, transcendentals=200000
        ),
        name="expert",
    )(rows, *pieces)


def pack_kernel(x_ref, gate_ref, up_ref, down_ref, *refs):
    outs, sems = refs[:X], refs[X]
    width = down_ref.shape[1]

    def copy(k, part):
        source = (gate_ref, up_ref, down_ref)[part]
        return pltpu.make_async_copy(
            source.at[(x_ref[0] + k) % X],
            outs[k].at[pl.ds(part * width, width)],
            sems.at[k, part],
        )

    for k in range(X):
        for part in range(3):
            copy(k, part).start()
    for k in range(X):
        for part in range(3):
            copy(k, part).wait()


def pack(x, gate_t, up_t, w_down):
    width = w_down.shape[1]
    hbm = pl.BlockSpec(memory_space=pl.ANY)
    return pl.pallas_call(
        pack_kernel,
        out_shape=[jax.ShapeDtypeStruct((3 * width, D), BF)] * X,
        in_specs=[pl.BlockSpec(memory_space=pltpu.SMEM), hbm, hbm, hbm],
        out_specs=[pl.BlockSpec(memory_space=pltpu.VMEM)] * X,
        scratch_shapes=[pltpu.SemaphoreType.DMA((X, 3))],
        cost_estimate=pl.CostEstimate(flops=0, bytes_accessed=9500000, transcendentals=0),
        name="pack",
    )(x.reshape(1).astype(jnp.int32), gate_t, up_t, w_down)


def spread(piece, axes, members):
    copies = jnp.broadcast_to(piece[None], (members, *piece.shape))
    return lax.all_to_all(copies, axes, 0, 0, tiled=True)


def turned(axis_size, by):
    return [(i, (i + by) % axis_size) for i in range(axis_size)]


def weight_pieces(w_gate, w_up, w_down, c, x, zl):
    packed = pack(x, jnp.swapaxes(w_gate, 1, 2), jnp.swapaxes(w_up, 1, 2), w_down)
    own = []
    for k in range(X):
        pairs = []
        for cs in range(C):
            for xs in range(X):
                for zs in range(ZL):
                    source = (cs * X + xs) * ZL + zs
                    target = (zs * X + (xs + k) % X) * ZL + cs
                    if source != target:
                        pairs.append((source, target))
        moved = lax.ppermute(packed[k], ("c", "x", "zl"), pairs)
        if k == 0:
            moved = jnp.where(zl == c, packed[k], moved)
        own.append(moved)
    other = []
    for k in range(X):
        other.append(lax.ppermute(own[k], "c", [(0, 1), (1, 0)]))
    return own + other


def on_device(
    tokens,
    attn_gain,
    w_query,
    w_key,
    w_value,
    query_gain,
    key_gain,
    w_out,
    moe_gain,
    expert_ids,
    expert_weights,
    w_gate,
    w_up,
    w_down,
):
    zh, y, c = lax.axis_index("zh"), lax.axis_index("y"), lax.axis_index("c")
    x, zl = lax.axis_index("x"), lax.axis_index("zl")
    sec = (zh * Y + y) * C + c
    narrow = x * ZL + zl
    local_rows = tokens.shape[0]
    share = local_rows // (X * ZL)
    positions = sec * local_rows + jnp.arange(local_rows, dtype=jnp.int32)
    cosine, sine = angles_of(positions)
    half = HEAD // 2

    pieces = weight_pieces(w_gate, w_up, w_down, c, x, zl)

    normed = rms_norm(tokens, attn_gain).astype(BF)

    def columns(w):
        turned_w = lax.dot_general(
            w, normed, (((0,), (1,)), ((), ())), preferred_element_type=F32
        )
        return jnp.swapaxes(turned_w.reshape(-1, KV_HEADS, local_rows), 0, 1)

    both = jnp.stack([columns(w_key), columns(w_value)], axis=1)
    both = both.reshape(X * ZL, -1, local_rows)
    one = lax.all_to_all(both, NARROW, 0, 0, tiled=True).reshape(HEAD, local_rows)
    key_t = one * lax.rsqrt(jnp.mean(one * one, axis=0, keepdims=True) + norm_eps)
    key_t = key_t * key_gain[:, None]
    cos_t, sin_t = cosine.T, sine.T
    lead, trail = key_t[:half], key_t[half:]
    key_t = jnp.concatenate(
        [lead * cos_t - trail * sin_t, trail * cos_t + lead * sin_t], axis=0
    ).astype(BF)
    piece = jnp.where(zl == 0, key_t, one.T.astype(BF))
    ring = spread(piece, ("zh", "zl"), ZH * ZL)
    own = spread(ring, "y", Y)
    own = own.reshape(Y, ZH, ZL, HEAD, HEAD)
    other = lax.ppermute(own, "c", [(0, 1), (1, 0)])

    query = jnp.dot(normed, w_query, preferred_element_type=F32).reshape(local_rows, -1, HEAD)
    query = rms_norm(query, query_gain)
    lead, trail = query[..., :half], query[..., half:]
    cos_q, sin_q = cosine[:, None, :], sine[:, None, :]
    query = jnp.concatenate(
        [lead * cos_q - trail * sin_q, trail * cos_q + lead * sin_q], axis=-1
    ).astype(BF)
    query = query.reshape(local_rows, -1)

    where = jnp.stack([zh * Y + y, c]).astype(jnp.int32)
    partial = attention(where, query, own, other, w_out)
    blocks = lax.all_to_all(partial.reshape(X * ZL, share, D), NARROW, 0, 0, tiled=True)
    mixed = jnp.sum(blocks.astype(F32), axis=0)
    own_tokens = lax.dynamic_slice_in_dim(tokens, narrow * share, share, 0)
    carried = (own_tokens.astype(F32) + mixed).astype(BF)
    moe_in = rms_norm(carried, moe_gain).astype(BF)

    ids = lax.dynamic_slice_in_dim(expert_ids, narrow * share, share, 0)
    weights = lax.dynamic_slice_in_dim(expert_weights, narrow * share, share, 0)
    gates = weights / jnp.sum(weights, axis=-1, keepdims=True)
    gates_high = gates.astype(BF)
    gates_low = (gates - gates_high.astype(F32)).astype(BF)
    tail = jnp.concatenate(
        [
            ids.astype(BF),
            gates_high,
            gates_low,
            jnp.zeros((share, 128 - 3 * TOPK), BF),
        ],
        axis=1,
    )
    packet = jnp.concatenate([moe_in, tail], axis=1)
    packets = [packet] + [lax.ppermute(packet, "zh", turned(ZH, k)) for k in range(1, ZH)]
    packets = jnp.concatenate(packets, axis=0)
    rows = packets[:, :D]
    routes = packets[:, D:].astype(F32)
    ids_f = routes[:, :TOPK]
    gates_all = routes[:, TOPK : 2 * TOPK] + routes[:, 2 * TOPK : 3 * TOPK]
    chips = jnp.arange(Y * X * ZL, dtype=jnp.int32)
    expert_of = (
        zh * (Y * X * ZL) + chips // (X * ZL) * (X * ZL) + chips % ZL * X + chips // ZL % X
    ).astype(F32)
    hits = ids_f[:, :, None] == expert_of[None, None, :]
    named = jnp.any(hits, axis=1).reshape(ZH, share, -1)
    gate_of = jnp.sum(jnp.where(hits, gates_all[:, :, None], 0.0), axis=1).reshape(ZH, share, -1)
    named_f = named.astype(F32)
    earlier = jnp.cumsum(named_f, axis=1) - named_f
    slot = jnp.arange(CAP, dtype=F32)
    chosen = named[..., None] & (earlier[..., None] == slot)
    same = jnp.eye(ZH, dtype=jnp.bool_)
    table = chosen[:, :, :, None, :] & same[:, None, None, :, None]
    table = table.reshape(ZH * share, -1)
    shared_gate = jnp.broadcast_to(
        gate_of[:, :, :, None, None], (ZH, share, Y * X * ZL, ZH, CAP)
    ).reshape(ZH * share, -1)
    outgoing = lax.dot_general(
        table.astype(BF), rows, (((0,), (0,)), ((), ())), preferred_element_type=F32
    ).astype(BF)
    arrived = lax.all_to_all(
        outgoing.reshape(Y * X * ZL, ZH * CAP, D), PLANE, 0, 0, tiled=True
    ).reshape(-1, D)
    answers = expert(arrived, pieces)
    returned = lax.all_to_all(
        answers.reshape(Y * X * ZL, ZH * CAP, D), PLANE, 0, 0, tiled=True
    ).reshape(-1, D)
    mixing = jnp.where(table, shared_gate, 0.0)
    mixing_high = mixing.astype(BF)
    mixing_low = (mixing - mixing_high.astype(F32)).astype(BF)
    sums = jnp.dot(mixing_high, returned, preferred_element_type=F32) + jnp.dot(
        mixing_low, returned, preferred_element_type=F32
    )
    sums = sums.reshape(ZH, share, D)
    result = carried.astype(F32) + sums[0]
    for k in range(1, ZH):
        back = lax.ppermute(sums[k].astype(BF), "zh", turned(ZH, -k))
        result = result + back.astype(F32)
    return result.astype(BF)


def solution(mesh):
    split = Mesh(mesh.devices.reshape(ZH, Y, C, X, ZL), ("zh", "y", "c", "x", "zl"))
    in_specs = (
        P(SEC, None),
        P(),
        P(None, NARROW),
        P(None, NARROW),
        P(None, NARROW),
        P(),
        P(),
        P(NARROW, None),
        P(),
        P(SEC, None),
        P(SEC, None),
        P(SEC, None, NARROW),
        P(SEC, None, NARROW),
        P(SEC, NARROW, None),
    )
    out_specs = P(SEC + NARROW, None)

    return jax.shard_map(
        on_device, mesh=split, in_specs=in_specs, out_specs=out_specs, check_vma=False
    )
```

```python
import math

import jax
import jax.numpy as jnp
from jax import lax
from jax.experimental import pallas as pl
from jax.experimental.pallas import tpu as pltpu
from jax.sharding import Mesh
from jax.sharding import PartitionSpec as P


D = 2048
KV_HEADS = 4
HEAD = 128
TOPK = 8
CAP = 2
SPAN = 512
ZH, Y, C, X, ZL = 4, 4, 2, 4, 2
SEC = ("zh", "y", "c")
NARROW = ("x", "zl")
PLANE = ("y", "x", "zl")

norm_eps = 1e-06
ATTEND_VMEM = 16 * 1024 * 1024
EXPERT_VMEM = 60 * 1024 * 1024
BF = jnp.bfloat16
F32 = jnp.float32


def rms_norm(inputs, gain):
    widened = inputs.astype(F32)
    return (
        widened * lax.rsqrt(jnp.mean(widened * widened, axis=-1, keepdims=True) + norm_eps) * gain
    )


def angles_of(positions):
    half = HEAD // 2
    inverse = jnp.exp(-jnp.log(1000000.0) * jnp.arange(half, dtype=F32) * 2.0 / HEAD)
    angles = positions.astype(F32)[:, None] * inverse[None, :]
    return jnp.cos(angles), jnp.sin(angles)


def attention_kernel(
    where_ref, q_ref, own_ref, other_ref, w_out_ref, out_ref, q_all, acc, peak, total, attended, out, sems
):
    rows = q_ref.shape[0]
    heads = q_ref.shape[1] // HEAD
    pair_here = where_ref[0]
    core = where_ref[1]
    factor = math.log2(math.e) / math.sqrt(HEAD)
    for h in range(heads):
        q_all[h * rows : (h + 1) * rows, :] = q_ref[:, h * HEAD : (h + 1) * HEAD]
    acc[...] = jnp.zeros_like(acc)
    total[...] = jnp.zeros_like(total)
    peak[...] = jnp.full_like(peak, -1e30)

    def step(group, last):
        zh = group // 2
        y = group % 2 * 2
        sources = ((own_ref, y), (other_ref, y), (own_ref, y + 1), (other_ref, y + 1))
        keys = jnp.concatenate([ref[at, zh, 0] for ref, at in sources], axis=1)
        values = jnp.concatenate([ref[at, zh, 1] for ref, at in sources], axis=0)
        s = jnp.dot(q_all[...], keys, preferred_element_type=F32)
        if last:
            row = lax.broadcasted_iota(jnp.int32, s.shape, 0) % rows
            column = lax.broadcasted_iota(jnp.int32, s.shape, 1)
            piece = column // HEAD
            section = 4 * group + piece // 2 * 2 + jnp.where(piece % 2 == 0, core, 1 - core)
            allowed = section * HEAD + column % HEAD <= (2 * pair_here + core) * rows + row
            s = jnp.where(allowed, s, -1e30)
        parts = [s[:, i * HEAD : (i + 1) * HEAD] for i in range(4)]
        highest = jnp.maximum(jnp.maximum(parts[0], parts[1]), jnp.maximum(parts[2], parts[3]))
        old = peak[...]
        new = jnp.maximum(old, jnp.max(highest, axis=-1, keepdims=True))
        p = jnp.exp2((s - new) * factor)
        if last:
            p = jnp.where(allowed, p, 0.0)
        parts = [p[:, i * HEAD : (i + 1) * HEAD] for i in range(4)]
        scale = jnp.exp2((old - new) * factor)
        total[...] = total[...] * scale + ((parts[0] + parts[1]) + (parts[2] + parts[3]))
        acc[...] = acc[...] * scale + jnp.dot(p.astype(BF), values, preferred_element_type=F32)
        peak[...] = new

    @pl.loop(0, pair_here // 2)
    def _(group):
        step(group, False)

    step(pair_here // 2, True)
    summed = jnp.sum(total[...], axis=-1, keepdims=True)
    for h in range(heads):
        part = slice(h * rows, (h + 1) * rows)
        attended[:, h * HEAD : (h + 1) * HEAD] = (acc[part, :] / summed[part]).astype(BF)
    copies = []
    for i in range(D // SPAN):
        out[i] = jnp.dot(
            attended[...], w_out_ref[:, i * SPAN : (i + 1) * SPAN], preferred_element_type=F32
        ).astype(BF)
        copies.append(
            pltpu.make_async_copy(out.at[i], out_ref.at[:, pl.ds(i * SPAN, SPAN)], sems.at[i])
        )
        copies[i].start()
    for copy in copies:
        copy.wait()


def attention(where, query, own, other, w_out):
    rows = query.shape[0]
    heads = query.shape[1] // HEAD
    vmem = pl.BlockSpec(memory_space=pltpu.VMEM)
    return pl.pallas_call(
        attention_kernel,
        out_shape=jax.ShapeDtypeStruct((rows, D), BF),
        in_specs=[pl.BlockSpec(memory_space=pltpu.SMEM), vmem, vmem, vmem, vmem],
        out_specs=pl.BlockSpec(memory_space=pltpu.HBM),
        scratch_shapes=[
            pltpu.VMEM((heads * rows, HEAD), BF),
            pltpu.VMEM((heads * rows, HEAD), F32),
            pltpu.VMEM((heads * rows, 1), F32),
            pltpu.VMEM((heads * rows, HEAD), F32),
            pltpu.VMEM((rows, heads * HEAD), BF),
            pltpu.VMEM((D // SPAN, rows, SPAN), BF),
            pltpu.SemaphoreType.DMA((D // SPAN,)),
        ],
        compiler_params=pltpu.CompilerParams(vmem_limit_bytes=ATTEND_VMEM),
        cost_estimate=pl.CostEstimate(
            flops=1400000000, bytes_accessed=5000000, transcendentals=2000000
        ),
        name="attend",
    )(where, query, own, other, w_out)


def expert_kernel(rows_ref, *refs):
    pieces = refs[:8]
    out_ref, weights, active, out, sems, out_sems = refs[8:]
    width = pieces[0].shape[0] // 3

    def fetch(part, i):
        return pltpu.make_async_copy(
            pieces[i].at[pl.ds(part * width, width)],
            weights.at[part, pl.ds(i * width, width)],
            sems.at[part, i],
        )

    for half in range(2):
        for part in range(2):
            for i in range(4):
                fetch(part, 4 * half + i).start()
    for i in range(8):
        fetch(2, i).start()
    rows = rows_ref[...]
    for half in range(2):
        for part in range(2):
            for i in range(4):
                fetch(part, 4 * half + i).wait()
        span = slice(4 * half * width, 4 * (half + 1) * width)
        gate = lax.dot_general(
            weights[0, span], rows, (((1,), (1,)), ((), ())), preferred_element_type=F32
        )
        up = lax.dot_general(
            weights[1, span], rows, (((1,), (1,)), ((), ())), preferred_element_type=F32
        )
        active[span, :] = (gate / (1.0 + jnp.exp(-gate)) * up).astype(BF)
    for i in range(8):
        fetch(2, i).wait()
    acts = active[...].T
    copies = []
    for i in range(D // SPAN):
        out[i] = jnp.dot(
            acts, weights[2, :, i * SPAN : (i + 1) * SPAN], preferred_element_type=F32
        ).astype(BF)
        copies.append(
            pltpu.make_async_copy(out.at[i], out_ref.at[:, pl.ds(i * SPAN, SPAN)], out_sems.at[i])
        )
        copies[i].start()
    for copy in copies:
        copy.wait()


def expert(rows, pieces):
    count = rows.shape[0]
    width = pieces[0].shape[0] // 3
    vmem = pl.BlockSpec(memory_space=pltpu.VMEM)
    hbm = pl.BlockSpec(memory_space=pl.ANY)
    return pl.pallas_call(
        expert_kernel,
        out_shape=jax.ShapeDtypeStruct((count, D), BF),
        in_specs=[vmem] + [hbm] * 8,
        out_specs=pl.BlockSpec(memory_space=pltpu.HBM),
        scratch_shapes=[
            pltpu.VMEM((3, 8 * width, D), BF),
            pltpu.VMEM((8 * width, count), BF),
            pltpu.VMEM((D // SPAN, count, SPAN), BF),
            pltpu.SemaphoreType.DMA((3, 8)),
            pltpu.SemaphoreType.DMA((D // SPAN,)),
        ],
        compiler_params=pltpu.CompilerParams(vmem_limit_bytes=EXPERT_VMEM),
        cost_estimate=pl.CostEstimate(
            flops=2400000000, bytes_accessed=11500000, transcendentals=200000
        ),
        name="expert",
    )(rows, *pieces)


def pack_kernel(x_ref, gate_ref, up_ref, down_ref, *refs):
    outs, sems = refs[:X], refs[X]
    width = down_ref.shape[1]

    def copy(k, part):
        source = (gate_ref, up_ref, down_ref)[part]
        return pltpu.make_async_copy(
            source.at[(x_ref[0] + k) % X],
            outs[k].at[pl.ds(part * width, width)],
            sems.at[k, part],
        )

    for k in range(X):
        for part in range(3):
            copy(k, part).start()
    for k in range(X):
        for part in range(3):
            copy(k, part).wait()


def pack(x, gate_t, up_t, w_down):
    width = w_down.shape[1]
    hbm = pl.BlockSpec(memory_space=pl.ANY)
    return pl.pallas_call(
        pack_kernel,
        out_shape=[jax.ShapeDtypeStruct((3 * width, D), BF)] * X,
        in_specs=[pl.BlockSpec(memory_space=pltpu.SMEM), hbm, hbm, hbm],
        out_specs=[pl.BlockSpec(memory_space=pltpu.VMEM)] * X,
        scratch_shapes=[pltpu.SemaphoreType.DMA((X, 3))],
        cost_estimate=pl.CostEstimate(flops=0, bytes_accessed=9500000, transcendentals=0),
        name="pack",
    )(x.reshape(1).astype(jnp.int32), gate_t, up_t, w_down)


def spread(piece, axes, members):
    copies = jnp.broadcast_to(piece[None], (members, *piece.shape))
    return lax.all_to_all(copies, axes, 0, 0, tiled=True)


def turned(axis_size, by):
    return [(i, (i + by) % axis_size) for i in range(axis_size)]


def weight_pieces(w_gate, w_up, w_down, c, x, zl):
    packed = pack(x, jnp.swapaxes(w_gate, 1, 2), jnp.swapaxes(w_up, 1, 2), w_down)
    own = []
    for k in range(X):
        pairs = []
        for cs in range(C):
            for xs in range(X):
                for zs in range(ZL):
                    source = (cs * X + xs) * ZL + zs
                    target = (zs * X + (xs + k) % X) * ZL + cs
                    if source != target:
                        pairs.append((source, target))
        moved = lax.ppermute(packed[k], ("c", "x", "zl"), pairs)
        if k == 0:
            moved = jnp.where(zl == c, packed[k], moved)
        own.append(moved)
    other = []
    for k in range(X):
        other.append(lax.ppermute(own[k], "c", [(0, 1), (1, 0)]))
    return own + other


def on_device(
    tokens,
    attn_gain,
    w_query,
    w_key,
    w_value,
    query_gain,
    key_gain,
    w_out,
    moe_gain,
    expert_ids,
    expert_weights,
    w_gate,
    w_up,
    w_down,
):
    zh, y, c = lax.axis_index("zh"), lax.axis_index("y"), lax.axis_index("c")
    x, zl = lax.axis_index("x"), lax.axis_index("zl")
    sec = (zh * Y + y) * C + c
    narrow = x * ZL + zl
    local_rows = tokens.shape[0]
    share = local_rows // (X * ZL)
    positions = sec * local_rows + jnp.arange(local_rows, dtype=jnp.int32)
    cosine, sine = angles_of(positions)
    half = HEAD // 2

    pieces = weight_pieces(w_gate, w_up, w_down, c, x, zl)

    normed = rms_norm(tokens, attn_gain).astype(BF)

    def columns(w):
        turned_w = lax.dot_general(
            w, normed, (((0,), (1,)), ((), ())), preferred_element_type=F32
        )
        return jnp.swapaxes(turned_w.reshape(-1, KV_HEADS, local_rows), 0, 1)

    both = jnp.stack([columns(w_key), columns(w_value)], axis=1)
    both = both.reshape(X * ZL, -1, local_rows)
    one = lax.all_to_all(both, NARROW, 0, 0, tiled=True).reshape(HEAD, local_rows)
    key_t = one * lax.rsqrt(jnp.mean(one * one, axis=0, keepdims=True) + norm_eps)
    key_t = key_t * key_gain[:, None]
    cos_t, sin_t = cosine.T, sine.T
    lead, trail = key_t[:half], key_t[half:]
    key_t = jnp.concatenate(
        [lead * cos_t - trail * sin_t, trail * cos_t + lead * sin_t], axis=0
    ).astype(BF)
    piece = jnp.where(zl == 0, key_t, one.T.astype(BF))
    ring = spread(piece, ("zh", "zl"), ZH * ZL)
    own = spread(ring, "y", Y)
    own = own.reshape(Y, ZH, ZL, HEAD, HEAD)
    other = lax.ppermute(own, "c", [(0, 1), (1, 0)])

    query = jnp.dot(normed, w_query, preferred_element_type=F32).reshape(local_rows, -1, HEAD)
    query = rms_norm(query, query_gain)
    lead, trail = query[..., :half], query[..., half:]
    cos_q, sin_q = cosine[:, None, :], sine[:, None, :]
    query = jnp.concatenate(
        [lead * cos_q - trail * sin_q, trail * cos_q + lead * sin_q], axis=-1
    ).astype(BF)
    query = query.reshape(local_rows, -1)

    where = jnp.stack([zh * Y + y, c]).astype(jnp.int32)
    partial = attention(where, query, own, other, w_out)
    blocks = lax.all_to_all(partial.reshape(X * ZL, share, D), NARROW, 0, 0, tiled=True)
    mixed = jnp.sum(blocks.astype(F32), axis=0)
    own_tokens = lax.dynamic_slice_in_dim(tokens, narrow * share, share, 0)
    carried = (own_tokens.astype(F32) + mixed).astype(BF)
    moe_in = rms_norm(carried, moe_gain).astype(BF)

    ids = lax.dynamic_slice_in_dim(expert_ids, narrow * share, share, 0)
    weights = lax.dynamic_slice_in_dim(expert_weights, narrow * share, share, 0)
    gates = weights / jnp.sum(weights, axis=-1, keepdims=True)
    gates_high = gates.astype(BF)
    gates_low = (gates - gates_high.astype(F32)).astype(BF)
    tail = jnp.concatenate(
        [
            ids.astype(BF),
            gates_high,
            gates_low,
            jnp.zeros((share, 128 - 3 * TOPK), BF),
        ],
        axis=1,
    )
    packet = jnp.concatenate([moe_in, tail], axis=1)
    packets = [packet] + [lax.ppermute(packet, "zh", turned(ZH, k)) for k in range(1, ZH)]
    packets = jnp.concatenate(packets, axis=0)
    rows = packets[:, :D]
    routes = packets[:, D:].astype(F32)
    ids_f = routes[:, :TOPK]
    gates_all = routes[:, TOPK : 2 * TOPK] + routes[:, 2 * TOPK : 3 * TOPK]
    chips = jnp.arange(Y * X * ZL, dtype=jnp.int32)
    expert_of = (
        zh * (Y * X * ZL) + chips // (X * ZL) * (X * ZL) + chips % ZL * X + chips // ZL % X
    ).astype(F32)
    hits = ids_f[:, :, None] == expert_of[None, None, :]
    named = jnp.any(hits, axis=1).reshape(ZH, share, -1)
    gate_of = jnp.sum(jnp.where(hits, gates_all[:, :, None], 0.0), axis=1).reshape(ZH, share, -1)
    named_f = named.astype(F32)
    earlier = jnp.cumsum(named_f, axis=1) - named_f
    slot = jnp.arange(CAP, dtype=F32)
    chosen = named[..., None] & (earlier[..., None] == slot)
    same = jnp.eye(ZH, dtype=jnp.bool_)
    table = chosen[:, :, :, None, :] & same[:, None, None, :, None]
    table = table.reshape(ZH * share, -1)
    shared_gate = jnp.broadcast_to(
        gate_of[:, :, :, None, None], (ZH, share, Y * X * ZL, ZH, CAP)
    ).reshape(ZH * share, -1)
    outgoing = lax.dot_general(
        table.astype(BF), rows, (((0,), (0,)), ((), ())), preferred_element_type=F32
    ).astype(BF)
    arrived = lax.all_to_all(
        outgoing.reshape(Y * X * ZL, ZH * CAP, D), PLANE, 0, 0, tiled=True
    ).reshape(-1, D)
    answers = expert(arrived, pieces)
    returned = lax.all_to_all(
        answers.reshape(Y * X * ZL, ZH * CAP, D), PLANE, 0, 0, tiled=True
    ).reshape(-1, D)
    mixing = jnp.where(table, shared_gate, 0.0)
    mixing_high = mixing.astype(BF)
    mixing_low = (mixing - mixing_high.astype(F32)).astype(BF)
    sums = jnp.dot(mixing_high, returned, preferred_element_type=F32) + jnp.dot(
        mixing_low, returned, preferred_element_type=F32
    )
    sums = sums.reshape(ZH, share, D)
    result = carried.astype(F32) + sums[0]
    for k in range(1, ZH):
        back = lax.ppermute(sums[k].astype(BF), "zh", turned(ZH, -k))
        result = result + back.astype(F32)
    return result.astype(BF)


def solution(mesh):
    split = Mesh(mesh.devices.reshape(ZH, Y, C, X, ZL), ("zh", "y", "c", "x", "zl"))
    in_specs = (
        P(SEC, None),
        P(),
        P(None, NARROW),
        P(None, NARROW),
        P(None, NARROW),
        P(),
        P(),
        P(NARROW, None),
        P(),
        P(SEC, None),
        P(SEC, None),
        P(SEC, None, NARROW),
        P(SEC, None, NARROW),
        P(SEC, NARROW, None),
    )
    out_specs = P(SEC + NARROW, None)

    return jax.shard_map(
        on_device, mesh=split, in_specs=in_specs, out_specs=out_specs, check_vma=False
    )
```

```python
import math

import jax
import jax.numpy as jnp
from jax import lax
from jax.experimental import pallas as pl
from jax.experimental.pallas import tpu as pltpu
from jax.sharding import Mesh
from jax.sharding import PartitionSpec as P


D = 2048
KV_HEADS = 4
HEAD = 128
TOPK = 8
CAP = 2
SPAN = 512
ZH, Y, C, X, ZL = 4, 4, 2, 4, 2
SEC = ("zh", "y", "c")
NARROW = ("x", "zl")
PLANE = ("y", "x", "zl")

norm_eps = 1e-06
ATTEND_VMEM = 16 * 1024 * 1024
EXPERT_VMEM = 60 * 1024 * 1024
BF = jnp.bfloat16
F32 = jnp.float32


def rms_norm(inputs, gain):
    widened = inputs.astype(F32)
    return (
        widened * lax.rsqrt(jnp.mean(widened * widened, axis=-1, keepdims=True) + norm_eps) * gain
    )


def angles_of(positions):
    half = HEAD // 2
    inverse = jnp.exp(-jnp.log(1000000.0) * jnp.arange(half, dtype=F32) * 2.0 / HEAD)
    angles = positions.astype(F32)[:, None] * inverse[None, :]
    return jnp.cos(angles), jnp.sin(angles)


def attention_kernel(
    where_ref, q_ref, own_ref, other_ref, w_out_ref, out_ref, q_all, acc, peak, total, attended, out, sems
):
    rows = q_ref.shape[0]
    heads = q_ref.shape[1] // HEAD
    pair_here = where_ref[0]
    core = where_ref[1]
    factor = math.log2(math.e) / math.sqrt(HEAD)
    for h in range(heads):
        q_all[h * rows : (h + 1) * rows, :] = q_ref[:, h * HEAD : (h + 1) * HEAD]
    acc[...] = jnp.zeros_like(acc)
    total[...] = jnp.zeros_like(total)
    peak[...] = jnp.full_like(peak, -1e30)

    def step(group, last):
        zh = group // 2
        y = group % 2 * 2
        sources = ((own_ref, y), (other_ref, y), (own_ref, y + 1), (other_ref, y + 1))
        keys = jnp.concatenate([ref[at, zh, 0] for ref, at in sources], axis=1)
        values = jnp.concatenate([ref[at, zh, 1] for ref, at in sources], axis=0)
        s = jnp.dot(q_all[...], keys, preferred_element_type=F32)
        if last:
            row = lax.broadcasted_iota(jnp.int32, s.shape, 0) % rows
            column = lax.broadcasted_iota(jnp.int32, s.shape, 1)
            piece = column // HEAD
            section = 4 * group + piece // 2 * 2 + jnp.where(piece % 2 == 0, core, 1 - core)
            allowed = section * HEAD + column % HEAD <= (2 * pair_here + core) * rows + row
            s = jnp.where(allowed, s, -1e30)
        parts = [s[:, i * HEAD : (i + 1) * HEAD] for i in range(4)]
        highest = jnp.maximum(jnp.maximum(parts[0], parts[1]), jnp.maximum(parts[2], parts[3]))
        old = peak[...]
        new = jnp.maximum(old, jnp.max(highest, axis=-1, keepdims=True))
        p = jnp.exp2((s - new) * factor)
        if last:
            p = jnp.where(allowed, p, 0.0)
        parts = [p[:, i * HEAD : (i + 1) * HEAD] for i in range(4)]
        scale = jnp.exp2((old - new) * factor)
        total[...] = total[...] * scale + ((parts[0] + parts[1]) + (parts[2] + parts[3]))
        acc[...] = acc[...] * scale + jnp.dot(p.astype(BF), values, preferred_element_type=F32)
        peak[...] = new

    @pl.loop(0, pair_here // 2)
    def _(group):
        step(group, False)

    step(pair_here // 2, True)
    summed = jnp.sum(total[...], axis=-1, keepdims=True)
    for h in range(heads):
        part = slice(h * rows, (h + 1) * rows)
        attended[:, h * HEAD : (h + 1) * HEAD] = (acc[part, :] / summed[part]).astype(BF)
    copies = []
    for i in range(D // SPAN):
        out[i] = jnp.dot(
            attended[...], w_out_ref[:, i * SPAN : (i + 1) * SPAN], preferred_element_type=F32
        ).astype(BF)
        copies.append(
            pltpu.make_async_copy(out.at[i], out_ref.at[:, pl.ds(i * SPAN, SPAN)], sems.at[i])
        )
        copies[i].start()
    for copy in copies:
        copy.wait()


def attention(where, query, own, other, w_out):
    rows = query.shape[0]
    heads = query.shape[1] // HEAD
    vmem = pl.BlockSpec(memory_space=pltpu.VMEM)
    return pl.pallas_call(
        attention_kernel,
        out_shape=jax.ShapeDtypeStruct((rows, D), BF),
        in_specs=[pl.BlockSpec(memory_space=pltpu.SMEM), vmem, vmem, vmem, vmem],
        out_specs=pl.BlockSpec(memory_space=pltpu.HBM),
        scratch_shapes=[
            pltpu.VMEM((heads * rows, HEAD), BF),
            pltpu.VMEM((heads * rows, HEAD), F32),
            pltpu.VMEM((heads * rows, 1), F32),
            pltpu.VMEM((heads * rows, HEAD), F32),
            pltpu.VMEM((rows, heads * HEAD), BF),
            pltpu.VMEM((D // SPAN, rows, SPAN), BF),
            pltpu.SemaphoreType.DMA((D // SPAN,)),
        ],
        compiler_params=pltpu.CompilerParams(vmem_limit_bytes=ATTEND_VMEM),
        cost_estimate=pl.CostEstimate(
            flops=1400000000, bytes_accessed=5000000, transcendentals=2000000
        ),
        name="attend",
    )(where, query, own, other, w_out)


def expert_kernel(rows_ref, *refs):
    pieces = refs[:8]
    out_ref, weights, active, out, sems, out_sems = refs[8:]
    width = pieces[0].shape[0] // 3

    def fetch(part, i):
        return pltpu.make_async_copy(
            pieces[i].at[pl.ds(part * width, width)],
            weights.at[part, pl.ds(i * width, width)],
            sems.at[part, i],
        )

    for half in range(2):
        for part in range(2):
            for i in range(4):
                fetch(part, 4 * half + i).start()
    for i in range(8):
        fetch(2, i).start()
    rows = rows_ref[...]
    for half in range(2):
        for part in range(2):
            for i in range(4):
                fetch(part, 4 * half + i).wait()
        span = slice(4 * half * width, 4 * (half + 1) * width)
        gate = lax.dot_general(
            weights[0, span], rows, (((1,), (1,)), ((), ())), preferred_element_type=F32
        )
        up = lax.dot_general(
            weights[1, span], rows, (((1,), (1,)), ((), ())), preferred_element_type=F32
        )
        active[span, :] = (gate / (1.0 + jnp.exp(-gate)) * up).astype(BF)
    for i in range(8):
        fetch(2, i).wait()
    acts = active[...].T
    copies = []
    for i in range(D // SPAN):
        out[i] = jnp.dot(
            acts, weights[2, :, i * SPAN : (i + 1) * SPAN], preferred_element_type=F32
        ).astype(BF)
        copies.append(
            pltpu.make_async_copy(out.at[i], out_ref.at[:, pl.ds(i * SPAN, SPAN)], out_sems.at[i])
        )
        copies[i].start()
    for copy in copies:
        copy.wait()


def expert(rows, pieces):
    count = rows.shape[0]
    width = pieces[0].shape[0] // 3
    vmem = pl.BlockSpec(memory_space=pltpu.VMEM)
    hbm = pl.BlockSpec(memory_space=pl.ANY)
    return pl.pallas_call(
        expert_kernel,
        out_shape=jax.ShapeDtypeStruct((count, D), BF),
        in_specs=[vmem] + [hbm] * 8,
        out_specs=pl.BlockSpec(memory_space=pltpu.HBM),
        scratch_shapes=[
            pltpu.VMEM((3, 8 * width, D), BF),
            pltpu.VMEM((8 * width, count), BF),
            pltpu.VMEM((D // SPAN, count, SPAN), BF),
            pltpu.SemaphoreType.DMA((3, 8)),
            pltpu.SemaphoreType.DMA((D // SPAN,)),
        ],
        compiler_params=pltpu.CompilerParams(vmem_limit_bytes=EXPERT_VMEM),
        cost_estimate=pl.CostEstimate(
            flops=2400000000, bytes_accessed=11500000, transcendentals=200000
        ),
        name="expert",
    )(rows, *pieces)


def pack_kernel(x_ref, gate_ref, up_ref, down_ref, *refs):
    outs, sems = refs[:X], refs[X]
    width = down_ref.shape[1]

    def copy(k, part):
        source = (gate_ref, up_ref, down_ref)[part]
        return pltpu.make_async_copy(
            source.at[(x_ref[0] + k) % X],
            outs[k].at[pl.ds(part * width, width)],
            sems.at[k, part],
        )

    for k in range(X):
        for part in range(3):
            copy(k, part).start()
    for k in range(X):
        for part in range(3):
            copy(k, part).wait()


def pack(x, gate_t, up_t, w_down):
    width = w_down.shape[1]
    hbm = pl.BlockSpec(memory_space=pl.ANY)
    return pl.pallas_call(
        pack_kernel,
        out_shape=[jax.ShapeDtypeStruct((3 * width, D), BF)] * X,
        in_specs=[pl.BlockSpec(memory_space=pltpu.SMEM), hbm, hbm, hbm],
        out_specs=[pl.BlockSpec(memory_space=pltpu.VMEM)] * X,
        scratch_shapes=[pltpu.SemaphoreType.DMA((X, 3))],
        cost_estimate=pl.CostEstimate(flops=0, bytes_accessed=9500000, transcendentals=0),
        name="pack",
    )(x.reshape(1).astype(jnp.int32), gate_t, up_t, w_down)


def spread(piece, axes, members):
    copies = jnp.broadcast_to(piece[None], (members, *piece.shape))
    return lax.all_to_all(copies, axes, 0, 0, tiled=True)


def turned(axis_size, by):
    return [(i, (i + by) % axis_size) for i in range(axis_size)]


def weight_pieces(w_gate, w_up, w_down, c, x, zl):
    packed = pack(x, jnp.swapaxes(w_gate, 1, 2), jnp.swapaxes(w_up, 1, 2), w_down)
    own = []
    for k in range(X):
        pairs = []
        for cs in range(C):
            for xs in range(X):
                for zs in range(ZL):
                    source = (cs * X + xs) * ZL + zs
                    target = (zs * X + (xs + k) % X) * ZL + cs
                    if source != target:
                        pairs.append((source, target))
        moved = lax.ppermute(packed[k], ("c", "x", "zl"), pairs)
        if k == 0:
            moved = jnp.where(zl == c, packed[k], moved)
        own.append(moved)
    other = []
    for k in range(X):
        other.append(lax.ppermute(own[k], "c", [(0, 1), (1, 0)]))
    return own + other


def on_device(
    tokens,
    attn_gain,
    w_query,
    w_key,
    w_value,
    query_gain,
    key_gain,
    w_out,
    moe_gain,
    expert_ids,
    expert_weights,
    w_gate,
    w_up,
    w_down,
):
    zh, y, c = lax.axis_index("zh"), lax.axis_index("y"), lax.axis_index("c")
    x, zl = lax.axis_index("x"), lax.axis_index("zl")
    sec = (zh * Y + y) * C + c
    narrow = x * ZL + zl
    local_rows = tokens.shape[0]
    share = local_rows // (X * ZL)
    positions = sec * local_rows + jnp.arange(local_rows, dtype=jnp.int32)
    cosine, sine = angles_of(positions)
    half = HEAD // 2

    pieces = weight_pieces(w_gate, w_up, w_down, c, x, zl)

    normed = rms_norm(tokens, attn_gain).astype(BF)

    def columns(w):
        turned_w = lax.dot_general(
            w, normed, (((0,), (1,)), ((), ())), preferred_element_type=F32
        )
        return jnp.swapaxes(turned_w.reshape(-1, KV_HEADS, local_rows), 0, 1)

    both = jnp.stack([columns(w_key), columns(w_value)], axis=1)
    both = both.reshape(X * ZL, -1, local_rows)
    one = lax.all_to_all(both, NARROW, 0, 0, tiled=True).reshape(HEAD, local_rows)
    key_t = one * lax.rsqrt(jnp.mean(one * one, axis=0, keepdims=True) + norm_eps)
    key_t = key_t * key_gain[:, None]
    cos_t, sin_t = cosine.T, sine.T
    lead, trail = key_t[:half], key_t[half:]
    key_t = jnp.concatenate(
        [lead * cos_t - trail * sin_t, trail * cos_t + lead * sin_t], axis=0
    ).astype(BF)
    piece = jnp.where(zl == 0, key_t, one.T.astype(BF))

    ids = lax.dynamic_slice_in_dim(expert_ids, narrow * share, share, 0)
    weights = lax.dynamic_slice_in_dim(expert_weights, narrow * share, share, 0)
    gates = weights / jnp.sum(weights, axis=-1, keepdims=True)
    gates_high = gates.astype(BF)
    gates_low = (gates - gates_high.astype(F32)).astype(BF)
    tail = jnp.concatenate(
        [ids.astype(BF), gates_high, gates_low, jnp.zeros((share, HEAD - 3 * TOPK), BF)], axis=1
    )
    ring = spread(jnp.concatenate([piece, tail], axis=0), ("zh", "zl"), ZH * ZL)
    tails = ring[:, HEAD:].reshape(ZH, ZL, share, HEAD)
    tails = lax.dynamic_index_in_dim(tails, zl, 1, keepdims=False)
    routes = jnp.concatenate(
        [lax.dynamic_index_in_dim(tails, (zh - k) % ZH, 0, keepdims=False) for k in range(ZH)],
        axis=0,
    ).astype(F32)
    ring = ring[:, :HEAD]
    own = spread(ring, "y", Y)
    own = own.reshape(Y, ZH, ZL, HEAD, HEAD)
    other = lax.ppermute(own, "c", [(0, 1), (1, 0)])

    query = jnp.dot(normed, w_query, preferred_element_type=F32).reshape(local_rows, -1, HEAD)
    query = rms_norm(query, query_gain)
    lead, trail = query[..., :half], query[..., half:]
    cos_q, sin_q = cosine[:, None, :], sine[:, None, :]
    query = jnp.concatenate(
        [lead * cos_q - trail * sin_q, trail * cos_q + lead * sin_q], axis=-1
    ).astype(BF)
    query = query.reshape(local_rows, -1)

    where = jnp.stack([zh * Y + y, c]).astype(jnp.int32)
    partial = attention(where, query, own, other, w_out)
    blocks = lax.all_to_all(partial.reshape(X * ZL, share, D), NARROW, 0, 0, tiled=True)
    mixed = jnp.sum(blocks.astype(F32), axis=0)
    own_tokens = lax.dynamic_slice_in_dim(tokens, narrow * share, share, 0)
    carried = (own_tokens.astype(F32) + mixed).astype(BF)
    moe_in = rms_norm(carried, moe_gain).astype(BF)

    rows = [moe_in] + [lax.ppermute(moe_in, "zh", turned(ZH, k)) for k in range(1, ZH)]
    rows = jnp.concatenate(rows, axis=0)
    ids_f = routes[:, :TOPK]
    gates_all = routes[:, TOPK : 2 * TOPK] + routes[:, 2 * TOPK : 3 * TOPK]
    chips = jnp.arange(Y * X * ZL, dtype=jnp.int32)
    expert_of = (
        zh * (Y * X * ZL) + chips // (X * ZL) * (X * ZL) + chips % ZL * X + chips // ZL % X
    ).astype(F32)
    hits = ids_f[:, :, None] == expert_of[None, None, :]
    named = jnp.any(hits, axis=1).reshape(ZH, share, -1)
    gate_of = jnp.sum(jnp.where(hits, gates_all[:, :, None], 0.0), axis=1).reshape(ZH, share, -1)
    named_f = named.astype(F32)
    earlier = jnp.cumsum(named_f, axis=1) - named_f
    slot = jnp.arange(CAP, dtype=F32)
    chosen = named[..., None] & (earlier[..., None] == slot)
    same = jnp.eye(ZH, dtype=jnp.bool_)
    table = chosen[:, :, :, None, :] & same[:, None, None, :, None]
    table = table.reshape(ZH * share, -1)
    shared_gate = jnp.broadcast_to(
        gate_of[:, :, :, None, None], (ZH, share, Y * X * ZL, ZH, CAP)
    ).reshape(ZH * share, -1)
    outgoing = lax.dot_general(
        table.astype(BF), rows, (((0,), (0,)), ((), ())), preferred_element_type=F32
    ).astype(BF)
    arrived = lax.all_to_all(
        outgoing.reshape(Y * X * ZL, ZH * CAP, D), PLANE, 0, 0, tiled=True
    ).reshape(-1, D)
    answers = expert(arrived, pieces)
    returned = lax.all_to_all(
        answers.reshape(Y * X * ZL, ZH * CAP, D), PLANE, 0, 0, tiled=True
    ).reshape(-1, D)
    mixing = jnp.where(table, shared_gate, 0.0)
    mixing_high = mixing.astype(BF)
    mixing_low = (mixing - mixing_high.astype(F32)).astype(BF)
    sums = jnp.dot(mixing_high, returned, preferred_element_type=F32) + jnp.dot(
        mixing_low, returned, preferred_element_type=F32
    )
    sums = sums.reshape(ZH, share, D)
    result = carried.astype(F32) + sums[0]
    for k in range(1, ZH):
        back = lax.ppermute(sums[k].astype(BF), "zh", turned(ZH, -k))
        result = result + back.astype(F32)
    return result.astype(BF)


def solution(mesh):
    split = Mesh(mesh.devices.reshape(ZH, Y, C, X, ZL), ("zh", "y", "c", "x", "zl"))
    in_specs = (
        P(SEC, None),
        P(),
        P(None, NARROW),
        P(None, NARROW),
        P(None, NARROW),
        P(),
        P(),
        P(NARROW, None),
        P(),
        P(SEC, None),
        P(SEC, None),
        P(SEC, None, NARROW),
        P(SEC, None, NARROW),
        P(SEC, NARROW, None),
    )
    out_specs = P(SEC + NARROW, None)

    return jax.shard_map(
        on_device, mesh=split, in_specs=in_specs, out_specs=out_specs, check_vma=False
    )
```

```python
import math

import jax
import jax.numpy as jnp
from jax import lax
from jax.experimental import pallas as pl
from jax.experimental.pallas import tpu as pltpu
from jax.sharding import Mesh
from jax.sharding import PartitionSpec as P


D = 2048
KV_HEADS = 4
HEAD = 128
TOPK = 8
CAP = 2
SPAN = 512
ZH, Y, C, X, ZL = 4, 4, 2, 4, 2
SEC = ("zh", "y", "c")
NARROW = ("x", "zl")
PLANE = ("y", "x", "zl")

norm_eps = 1e-06
EXPERT_VMEM = 60 * 1024 * 1024
BF = jnp.bfloat16
F32 = jnp.float32


def rms_norm(inputs, gain):
    widened = inputs.astype(F32)
    return (
        widened * lax.rsqrt(jnp.mean(widened * widened, axis=-1, keepdims=True) + norm_eps) * gain
    )


def angles_of(positions):
    half = HEAD // 2
    inverse = jnp.exp(-jnp.log(1000000.0) * jnp.arange(half, dtype=F32) * 2.0 / HEAD)
    angles = positions.astype(F32)[:, None] * inverse[None, :]
    return jnp.cos(angles), jnp.sin(angles)


def attention_kernel(
    where_ref, q_ref, cos_ref, sin_ref, gain_ref, own_ref, other_ref, w_out_ref, out_ref, q_all, acc, peak, total, attended, w_out, sem
):
    rows = q_ref.shape[0]
    heads = q_ref.shape[1] // HEAD
    pair_here, core = where_ref[0], where_ref[1]
    factor = math.log2(math.e) / math.sqrt(HEAD)
    fetch = pltpu.make_async_copy(w_out_ref, w_out, sem)
    fetch.start()
    for h in range(heads):
        q = q_ref[:, h * HEAD : (h + 1) * HEAD]
        q = q * lax.rsqrt(jnp.mean(q * q, axis=-1, keepdims=True) + norm_eps) * gain_ref[...]
        q = q * cos_ref[...] + pltpu.roll(q, HEAD // 2, 1) * sin_ref[...]
        q_all[h * rows : (h + 1) * rows, :] = q.astype(BF)
    acc[...] = jnp.zeros_like(acc)
    total[...] = jnp.zeros_like(total)
    peak[...] = jnp.full_like(peak, -1e30)

    def step(group, last):
        zh = group // 2
        y = group % 2 * 2
        sources = ((own_ref, y), (other_ref, y), (own_ref, y + 1), (other_ref, y + 1))
        keys = jnp.concatenate([ref[at, zh, 0] for ref, at in sources], axis=1)
        values = jnp.concatenate([ref[at, zh, 1] for ref, at in sources], axis=0)
        s = jnp.dot(q_all[...], keys, preferred_element_type=F32)
        if last:
            row = lax.broadcasted_iota(jnp.int32, s.shape, 0) % rows
            column = lax.broadcasted_iota(jnp.int32, s.shape, 1)
            piece = column // HEAD
            section = 4 * group + piece // 2 * 2 + jnp.where(piece % 2 == 0, core, 1 - core)
            allowed = section * HEAD + column % HEAD <= (2 * pair_here + core) * rows + row
            s = jnp.where(allowed, s, -1e30)
        parts = [s[:, i * HEAD : (i + 1) * HEAD] for i in range(4)]
        highest = jnp.maximum(jnp.maximum(parts[0], parts[1]), jnp.maximum(parts[2], parts[3]))
        old = peak[...]
        new = jnp.maximum(old, jnp.max(highest, axis=-1, keepdims=True))
        p = jnp.exp2((s - new) * factor)
        if last:
            p = jnp.where(allowed, p, 0.0)
        parts = [p[:, i * HEAD : (i + 1) * HEAD] for i in range(4)]
        scale = jnp.exp2((old - new) * factor)
        total[...] = total[...] * scale + ((parts[0] + parts[1]) + (parts[2] + parts[3]))
        acc[...] = acc[...] * scale + jnp.dot(p.astype(BF), values, preferred_element_type=F32)
        peak[...] = new

    @pl.loop(0, pair_here // 2)
    def _(group):
        step(group, False)

    step(pair_here // 2, True)
    summed = jnp.sum(total[...], axis=-1, keepdims=True)
    for h in range(heads):
        part = slice(h * rows, (h + 1) * rows)
        attended[:, h * HEAD : (h + 1) * HEAD] = (acc[part, :] / summed[part]).astype(BF)
    fetch.wait()
    for i in range(D // SPAN):
        part = slice(i * SPAN, (i + 1) * SPAN)
        out_ref[:, part] = jnp.dot(
            attended[...], w_out[:, part], preferred_element_type=F32
        ).astype(BF)


def attention(where, query, cosine, sine, gain, own, other, w_out):
    rows = query.shape[0]
    heads = query.shape[1] // HEAD
    vmem = pl.BlockSpec(memory_space=pltpu.VMEM)
    return pl.pallas_call(
        attention_kernel,
        out_shape=jax.ShapeDtypeStruct((rows, D), BF),
        in_specs=[pl.BlockSpec(memory_space=pltpu.SMEM)]
        + [vmem] * 6
        + [pl.BlockSpec(memory_space=pl.ANY)],
        out_specs=vmem,
        scratch_shapes=[
            pltpu.VMEM((heads * rows, HEAD), BF),
            pltpu.VMEM((heads * rows, HEAD), F32),
            pltpu.VMEM((heads * rows, 1), F32),
            pltpu.VMEM((heads * rows, HEAD), F32),
            pltpu.VMEM((rows, heads * HEAD), BF),
            pltpu.VMEM(w_out.shape, BF),
            pltpu.SemaphoreType.DMA,
        ],
        cost_estimate=pl.CostEstimate(
            flops=1400000000, bytes_accessed=5000000, transcendentals=2000000
        ),
        name="attend",
    )(where, query, cosine, sine, gain, own, other, w_out)


def carry_kernel(blocks_ref, tokens_ref, gain_ref, carried_ref, normed_ref):
    mixed = jnp.sum(blocks_ref[...].astype(F32), axis=0)
    carried = (tokens_ref[...].astype(F32) + mixed).astype(BF)
    carried_ref[...] = carried
    normed_ref[...] = rms_norm(carried, gain_ref[...]).astype(BF)


def carry(blocks, tokens, gain):
    vmem = pl.BlockSpec(memory_space=pltpu.VMEM)
    shape = jax.ShapeDtypeStruct(tokens.shape, BF)
    return pl.pallas_call(
        carry_kernel,
        out_shape=[shape, shape],
        in_specs=[vmem] * 3,
        out_specs=[vmem] * 2,
        cost_estimate=pl.CostEstimate(flops=600000, bytes_accessed=800000, transcendentals=16),
        name="carry",
    )(blocks, tokens, gain.reshape(1, -1))


def route_kernel(where_ref, ring_ref, *refs):
    rows, (out_ref, high_ref, low_ref) = refs[:ZH], refs[ZH:]
    zh, zl = where_ref[0], where_ref[1]
    share = rows[0].shape[0]
    tails = jnp.concatenate(
        [ring_ref[(zh + ZH - k) % ZH * ZL + zl, HEAD:, :] for k in range(ZH)], axis=0
    ).astype(F32)
    shape = (ZH * share, Y * X * ZL * ZH * CAP)
    row = lax.broadcasted_iota(jnp.int32, shape, 0)
    column = lax.broadcasted_iota(jnp.int32, shape, 1)
    slot, source, chip = column % CAP, column // CAP % ZH, column // (CAP * ZH)
    expert_of = (
        zh * (Y * X * ZL) + chip // (X * ZL) * (X * ZL) + chip % ZL * X + chip // ZL % X
    ).astype(F32)
    hits = jnp.zeros(shape, F32)
    gate = jnp.zeros(shape, F32)
    for k in range(TOPK):
        same = tails[:, k : k + 1] == expert_of
        weight = tails[:, TOPK + k : TOPK + k + 1] + tails[:, 2 * TOPK + k : 2 * TOPK + k + 1]
        hits = jnp.where(same, 1.0, hits)
        gate = jnp.where(same, weight, gate)
    one = lax.broadcasted_iota(jnp.int32, (ZH * share, ZH * share), 0)
    two = lax.broadcasted_iota(jnp.int32, (ZH * share, ZH * share), 1)
    before = jnp.where(jnp.logical_and(two < one, two // share == one // share), 1.0, 0.0)
    earlier = jnp.dot(before.astype(BF), hits.astype(BF), preferred_element_type=F32)
    placed = jnp.logical_and(source == row // share, earlier == slot.astype(F32))
    table = jnp.where(placed, hits, 0.0)
    mixing = table * gate
    high = mixing.astype(BF)
    high_ref[...] = high
    low_ref[...] = (mixing - high.astype(F32)).astype(BF)
    whole = jnp.concatenate([ref[...] for ref in rows], axis=0)
    turned_table = table.T.astype(BF)
    for i in range(D // SPAN):
        part = slice(i * SPAN, (i + 1) * SPAN)
        out_ref[:, part] = jnp.dot(
            turned_table, whole[:, part], preferred_element_type=F32
        ).astype(BF)


def route(where, ring, rows):
    vmem = pl.BlockSpec(memory_space=pltpu.VMEM)
    slots = Y * X * ZL * ZH * CAP
    count = sum(r.shape[0] for r in rows)
    return pl.pallas_call(
        route_kernel,
        out_shape=[
            jax.ShapeDtypeStruct((slots, D), BF),
            jax.ShapeDtypeStruct((count, slots), BF),
            jax.ShapeDtypeStruct((count, slots), BF),
        ],
        in_specs=[pl.BlockSpec(memory_space=pltpu.SMEM)] + [vmem] * (1 + len(rows)),
        out_specs=[vmem] * 3,
        cost_estimate=pl.CostEstimate(flops=70000000, bytes_accessed=1700000, transcendentals=0),
        name="route",
    )(where, ring, *rows)


def expert_kernel(rows_ref, *refs):
    pieces = refs[:8]
    out_ref, weights, active, out, sems, out_sems = refs[8:]
    width = pieces[0].shape[0] // 3

    def fetch(part, i):
        return pltpu.make_async_copy(
            pieces[i].at[pl.ds(part * width, width)],
            weights.at[part, pl.ds(i * width, width)],
            sems.at[part, i],
        )

    for half in range(2):
        for part in range(2):
            for i in range(4):
                fetch(part, 4 * half + i).start()
    for i in range(8):
        fetch(2, i).start()
    rows = rows_ref[...]
    for half in range(2):
        for part in range(2):
            for i in range(4):
                fetch(part, 4 * half + i).wait()
        span = slice(4 * half * width, 4 * (half + 1) * width)
        gate = lax.dot_general(
            weights[0, span], rows, (((1,), (1,)), ((), ())), preferred_element_type=F32
        )
        up = lax.dot_general(
            weights[1, span], rows, (((1,), (1,)), ((), ())), preferred_element_type=F32
        )
        active[span, :] = (gate / (1.0 + jnp.exp(-gate)) * up).astype(BF)
    for i in range(8):
        fetch(2, i).wait()
    acts = active[...].T
    copies = []
    for i in range(D // SPAN):
        out[i] = jnp.dot(
            acts, weights[2, :, i * SPAN : (i + 1) * SPAN], preferred_element_type=F32
        ).astype(BF)
        copies.append(
            pltpu.make_async_copy(out.at[i], out_ref.at[:, pl.ds(i * SPAN, SPAN)], out_sems.at[i])
        )
        copies[i].start()
    for copy in copies:
        copy.wait()


def expert(rows, pieces):
    count = rows.shape[0]
    width = pieces[0].shape[0] // 3
    vmem = pl.BlockSpec(memory_space=pltpu.VMEM)
    hbm = pl.BlockSpec(memory_space=pl.ANY)
    return pl.pallas_call(
        expert_kernel,
        out_shape=jax.ShapeDtypeStruct((count, D), BF),
        in_specs=[vmem] + [hbm] * 8,
        out_specs=pl.BlockSpec(memory_space=pltpu.HBM),
        scratch_shapes=[
            pltpu.VMEM((3, 8 * width, D), BF),
            pltpu.VMEM((8 * width, count), BF),
            pltpu.VMEM((D // SPAN, count, SPAN), BF),
            pltpu.SemaphoreType.DMA((3, 8)),
            pltpu.SemaphoreType.DMA((D // SPAN,)),
        ],
        compiler_params=pltpu.CompilerParams(vmem_limit_bytes=EXPERT_VMEM),
        cost_estimate=pl.CostEstimate(
            flops=2400000000, bytes_accessed=11500000, transcendentals=200000
        ),
        name="expert",
    )(rows, *pieces)


def pack_kernel(x_ref, gate_ref, up_ref, down_ref, *refs):
    outs, sems = refs[:X], refs[X]
    width = down_ref.shape[1]

    def copy(k, part):
        source = (gate_ref, up_ref, down_ref)[part]
        return pltpu.make_async_copy(
            source.at[(x_ref[0] + k) % X],
            outs[k].at[pl.ds(part * width, width)],
            sems.at[k, part],
        )

    for k in range(X):
        for part in range(3):
            copy(k, part).start()
    for k in range(X):
        for part in range(3):
            copy(k, part).wait()


def pack(x, gate_t, up_t, w_down):
    width = w_down.shape[1]
    hbm = pl.BlockSpec(memory_space=pl.ANY)
    return pl.pallas_call(
        pack_kernel,
        out_shape=[jax.ShapeDtypeStruct((3 * width, D), BF)] * X,
        in_specs=[pl.BlockSpec(memory_space=pltpu.SMEM), hbm, hbm, hbm],
        out_specs=[pl.BlockSpec(memory_space=pltpu.VMEM)] * X,
        scratch_shapes=[pltpu.SemaphoreType.DMA((X, 3))],
        cost_estimate=pl.CostEstimate(flops=0, bytes_accessed=9500000, transcendentals=0),
        name="pack",
    )(x.reshape(1).astype(jnp.int32), gate_t, up_t, w_down)


def spread(piece, axes, members):
    copies = jnp.broadcast_to(piece[None], (members, *piece.shape))
    return lax.all_to_all(copies, axes, 0, 0, tiled=True)


def turned(axis_size, by):
    return [(i, (i + by) % axis_size) for i in range(axis_size)]


def weight_pieces(w_gate, w_up, w_down, c, x, zl):
    packed = pack(x, jnp.swapaxes(w_gate, 1, 2), jnp.swapaxes(w_up, 1, 2), w_down)

    def shifted(k, straight):
        return [
            ((cs * X + xs) * ZL + zs, (zs * X + (xs + k) % X) * ZL + cs)
            for cs in range(C)
            for xs in range(X)
            for zs in range(ZL)
            if (cs == zs) == straight
        ]

    own = []
    for k in range(X):
        straight = packed[0]
        if k > 0:
            straight = lax.ppermute(packed[k], ("c", "x", "zl"), shifted(k, True))
        crossed = lax.ppermute(packed[k], ("c", "x", "zl"), shifted(k, False))
        own.append(jnp.where(zl == c, straight, crossed))
    other = []
    for k in range(X):
        other.append(lax.ppermute(own[k], "c", [(0, 1), (1, 0)]))
    return own + other


def on_device(
    tokens,
    attn_gain,
    w_query,
    w_key,
    w_value,
    query_gain,
    key_gain,
    w_out,
    moe_gain,
    expert_ids,
    expert_weights,
    w_gate,
    w_up,
    w_down,
):
    zh, y, c = lax.axis_index("zh"), lax.axis_index("y"), lax.axis_index("c")
    x, zl = lax.axis_index("x"), lax.axis_index("zl")
    sec = (zh * Y + y) * C + c
    narrow = x * ZL + zl
    local_rows = tokens.shape[0]
    share = local_rows // (X * ZL)
    positions = sec * local_rows + jnp.arange(local_rows, dtype=jnp.int32)
    cosine, sine = angles_of(positions)
    half = HEAD // 2

    pieces = weight_pieces(w_gate, w_up, w_down, c, x, zl)

    normed = rms_norm(tokens, attn_gain).astype(BF)

    def columns(w):
        turned_w = lax.dot_general(
            w, normed, (((0,), (1,)), ((), ())), preferred_element_type=F32
        )
        return jnp.swapaxes(turned_w.reshape(-1, KV_HEADS, local_rows), 0, 1)

    both = jnp.stack([columns(w_key), columns(w_value)], axis=1)
    both = both.reshape(X * ZL, -1, local_rows)
    one = lax.all_to_all(both, NARROW, 0, 0, tiled=True).reshape(HEAD, local_rows)
    key_t = one * lax.rsqrt(jnp.mean(one * one, axis=0, keepdims=True) + norm_eps)
    key_t = key_t * key_gain[:, None]
    cos_t, sin_t = cosine.T, sine.T
    lead, trail = key_t[:half], key_t[half:]
    key_t = jnp.concatenate(
        [lead * cos_t - trail * sin_t, trail * cos_t + lead * sin_t], axis=0
    ).astype(BF)
    piece = jnp.where(zl == 0, key_t, one.T.astype(BF))

    ids = lax.dynamic_slice_in_dim(expert_ids, narrow * share, share, 0)
    weights = lax.dynamic_slice_in_dim(expert_weights, narrow * share, share, 0)
    gates = weights / jnp.sum(weights, axis=-1, keepdims=True)
    gates_high = gates.astype(BF)
    gates_low = (gates - gates_high.astype(F32)).astype(BF)
    tail = jnp.concatenate(
        [ids.astype(BF), gates_high, gates_low, jnp.zeros((share, HEAD - 3 * TOPK), BF)], axis=1
    )
    ring = spread(jnp.concatenate([piece, tail], axis=0), ("zh", "zl"), ZH * ZL)
    own = spread(ring[:, :HEAD], "y", Y)
    own = own.reshape(Y, ZH, ZL, HEAD, HEAD)
    other = lax.ppermute(own, "c", [(0, 1), (1, 0)])

    query = jnp.dot(normed, w_query, preferred_element_type=F32)
    where = jnp.stack([zh * Y + y, c]).astype(jnp.int32)
    place = jnp.stack([zh, zl]).astype(jnp.int32)
    cosines = jnp.concatenate([cosine, cosine], axis=1)
    sines = jnp.concatenate([-sine, sine], axis=1)
    partial = attention(
        where, query, cosines, sines, query_gain.reshape(1, -1), own, other, w_out
    )
    partial, tokens = lax.optimization_barrier((partial, tokens))
    blocks = lax.all_to_all(partial.reshape(X * ZL, share, D), NARROW, 0, 0, tiled=True)
    own_tokens = lax.dynamic_slice_in_dim(tokens, narrow * share, share, 0)
    carried, moe_in = carry(blocks, own_tokens, moe_gain)

    rows = [moe_in] + [lax.ppermute(moe_in, "zh", turned(ZH, k)) for k in range(1, ZH)]
    outgoing, mixing_high, mixing_low = route(place, ring, rows)
    arrived = lax.all_to_all(
        outgoing.reshape(Y * X * ZL, ZH * CAP, D), PLANE, 0, 0, tiled=True
    ).reshape(-1, D)
    answers = expert(arrived, pieces)
    returned = lax.all_to_all(
        answers.reshape(Y * X * ZL, ZH * CAP, D), PLANE, 0, 0, tiled=True
    ).reshape(-1, D)
    sums = jnp.dot(mixing_high, returned, preferred_element_type=F32) + jnp.dot(
        mixing_low, returned, preferred_element_type=F32
    )
    sums = sums.reshape(ZH, share, D)
    result = carried.astype(F32) + sums[0]
    for k in range(1, ZH):
        back = lax.ppermute(sums[k].astype(BF), "zh", turned(ZH, -k))
        result = result + back.astype(F32)
    return result.astype(BF)


def solution(mesh):
    split = Mesh(mesh.devices.reshape(ZH, Y, C, X, ZL), ("zh", "y", "c", "x", "zl"))
    in_specs = (
        P(SEC, None),
        P(),
        P(None, NARROW),
        P(None, NARROW),
        P(None, NARROW),
        P(),
        P(),
        P(NARROW, None),
        P(),
        P(SEC, None),
        P(SEC, None),
        P(SEC, None, NARROW),
        P(SEC, None, NARROW),
        P(SEC, NARROW, None),
    )
    out_specs = P(SEC + NARROW, None)

    return jax.shard_map(
        on_device, mesh=split, in_specs=in_specs, out_specs=out_specs, check_vma=False
    )
```

```python
import functools
import math

import jax
import jax.numpy as jnp
from jax import lax
from jax.experimental import pallas as pl
from jax.experimental.pallas import tpu as pltpu
from jax.sharding import Mesh
from jax.sharding import PartitionSpec as P


D = 2048
KV_HEADS = 4
HEAD = 128
TOPK = 8
CAP = 2
SPAN = 512
ZH, Y, C, X, ZL = 4, 4, 2, 4, 2
SEC = ("zh", "y", "c")
NARROW = ("x", "zl")
PLANE = ("y", "x", "zl")

norm_eps = 1e-06
SPLIT = (2,)
EXPERT_VMEM = 60 * 1024 * 1024
BF = jnp.bfloat16
F32 = jnp.float32


def rms_norm(inputs, gain):
    widened = inputs.astype(F32)
    return (
        widened * lax.rsqrt(jnp.mean(widened * widened, axis=-1, keepdims=True) + norm_eps) * gain
    )


def angles_of(positions):
    half = HEAD // 2
    inverse = jnp.exp(-jnp.log(1000000.0) * jnp.arange(half, dtype=F32) * 2.0 / HEAD)
    angles = positions.astype(F32)[:, None] * inverse[None, :]
    return jnp.cos(angles), jnp.sin(angles)


def attention_kernel(
    where_ref, q_ref, cos_ref, sin_ref, gain_ref, own_ref, other_ref, w_out_ref, out_ref, q_all, acc, peak, total, attended, w_out, sem
):
    rows = q_ref.shape[0]
    heads = q_ref.shape[1] // HEAD
    pair_here, core = where_ref[0], where_ref[1]
    factor = math.log2(math.e) / math.sqrt(HEAD)
    fetch = pltpu.make_async_copy(w_out_ref, w_out, sem)
    fetch.start()
    for h in range(heads):
        q = q_ref[:, h * HEAD : (h + 1) * HEAD]
        q = q * lax.rsqrt(jnp.mean(q * q, axis=-1, keepdims=True) + norm_eps) * gain_ref[...]
        q = q * cos_ref[...] + pltpu.roll(q, HEAD // 2, 1) * sin_ref[...]
        q_all[h * rows : (h + 1) * rows, :] = q.astype(BF)
    acc[...] = jnp.zeros_like(acc)
    total[...] = jnp.zeros_like(total)
    peak[...] = jnp.full_like(peak, -1e30)

    def step(group, last):
        zh = group // 2
        y = group % 2 * 2
        sources = ((own_ref, y), (other_ref, y), (own_ref, y + 1), (other_ref, y + 1))
        keys = jnp.concatenate([ref[at, zh, 0] for ref, at in sources], axis=1)
        values = jnp.concatenate([ref[at, zh, 1] for ref, at in sources], axis=0)
        s = jnp.dot(q_all[...], keys, preferred_element_type=F32)
        if last:
            row = lax.broadcasted_iota(jnp.int32, s.shape, 0) % rows
            column = lax.broadcasted_iota(jnp.int32, s.shape, 1)
            piece = column // HEAD
            section = 4 * group + piece // 2 * 2 + jnp.where(piece % 2 == 0, core, 1 - core)
            allowed = section * HEAD + column % HEAD <= (2 * pair_here + core) * rows + row
            s = jnp.where(allowed, s, -1e30)
        parts = [s[:, i * HEAD : (i + 1) * HEAD] for i in range(4)]
        highest = jnp.maximum(jnp.maximum(parts[0], parts[1]), jnp.maximum(parts[2], parts[3]))
        old = peak[...]
        new = jnp.maximum(old, jnp.max(highest, axis=-1, keepdims=True))
        p = jnp.exp2((s - new) * factor)
        if last:
            p = jnp.where(allowed, p, 0.0)
        parts = [p[:, i * HEAD : (i + 1) * HEAD] for i in range(4)]
        scale = jnp.exp2((old - new) * factor)
        total[...] = total[...] * scale + ((parts[0] + parts[1]) + (parts[2] + parts[3]))
        acc[...] = acc[...] * scale + jnp.dot(p.astype(BF), values, preferred_element_type=F32)
        peak[...] = new

    @pl.loop(0, pair_here // 2)
    def _(group):
        step(group, False)

    step(pair_here // 2, True)
    summed = jnp.sum(total[...], axis=-1, keepdims=True)
    for h in range(heads):
        part = slice(h * rows, (h + 1) * rows)
        attended[:, h * HEAD : (h + 1) * HEAD] = (acc[part, :] / summed[part]).astype(BF)
    fetch.wait()
    for i in range(D // SPAN):
        part = slice(i * SPAN, (i + 1) * SPAN)
        out_ref[:, part] = jnp.dot(
            attended[...], w_out[:, part], preferred_element_type=F32
        ).astype(BF)


def attention(where, query, cosine, sine, gain, own, other, w_out):
    rows = query.shape[0]
    heads = query.shape[1] // HEAD
    vmem = pl.BlockSpec(memory_space=pltpu.VMEM)
    return pl.pallas_call(
        attention_kernel,
        out_shape=jax.ShapeDtypeStruct((rows, D), BF),
        in_specs=[pl.BlockSpec(memory_space=pltpu.SMEM)]
        + [vmem] * 6
        + [pl.BlockSpec(memory_space=pl.ANY)],
        out_specs=vmem,
        scratch_shapes=[
            pltpu.VMEM((heads * rows, HEAD), BF),
            pltpu.VMEM((heads * rows, HEAD), F32),
            pltpu.VMEM((heads * rows, 1), F32),
            pltpu.VMEM((heads * rows, HEAD), F32),
            pltpu.VMEM((rows, heads * HEAD), BF),
            pltpu.VMEM(w_out.shape, BF),
            pltpu.SemaphoreType.DMA,
        ],
        cost_estimate=pl.CostEstimate(
            flops=1400000000, bytes_accessed=5000000, transcendentals=2000000
        ),
        name="attend",
    )(where, query, cosine, sine, gain, own, other, w_out)


def carry_kernel(blocks_ref, tokens_ref, gain_ref, carried_ref, normed_ref):
    mixed = jnp.sum(blocks_ref[...].astype(F32), axis=0)
    carried = (tokens_ref[...].astype(F32) + mixed).astype(BF)
    carried_ref[...] = carried
    normed_ref[...] = rms_norm(carried, gain_ref[...]).astype(BF)


def carry(blocks, tokens, gain):
    vmem = pl.BlockSpec(memory_space=pltpu.VMEM)
    shape = jax.ShapeDtypeStruct(tokens.shape, BF)
    return pl.pallas_call(
        carry_kernel,
        out_shape=[shape, shape],
        in_specs=[vmem] * 3,
        out_specs=[vmem] * 2,
        cost_estimate=pl.CostEstimate(flops=600000, bytes_accessed=800000, transcendentals=16),
        name="carry",
    )(blocks, tokens, gain.reshape(1, -1))


def table_kernel(gates, where_ref, ring_ref, table_ref):
    zh, zl = where_ref[0], where_ref[1]
    share = ring_ref.shape[1] - HEAD
    tails = jnp.concatenate(
        [ring_ref[(zh + ZH - k) % ZH * ZL + zl, HEAD:, :] for k in range(ZH)], axis=0
    ).astype(F32)
    shape = (ZH * share, Y * X * ZL * ZH * CAP)
    row = lax.broadcasted_iota(jnp.int32, shape, 0)
    column = lax.broadcasted_iota(jnp.int32, shape, 1)
    slot, source, chip = column % CAP, column // CAP % ZH, column // (CAP * ZH)
    expert_of = (
        zh * (Y * X * ZL) + chip // (X * ZL) * (X * ZL) + chip % ZL * X + chip // ZL % X
    ).astype(F32)
    hits = jnp.zeros(shape, F32)
    gate = jnp.zeros(shape, F32)
    for k in range(TOPK):
        same = tails[:, k : k + 1] == expert_of
        weight = tails[:, TOPK + k : TOPK + k + 1] + tails[:, 2 * TOPK + k : 2 * TOPK + k + 1]
        hits = jnp.where(same, 1.0, hits)
        gate = jnp.where(same, weight, gate)
    one = lax.broadcasted_iota(jnp.int32, (ZH * share, ZH * share), 0)
    two = lax.broadcasted_iota(jnp.int32, (ZH * share, ZH * share), 1)
    before = jnp.where(jnp.logical_and(two < one, two // share == one // share), 1.0, 0.0)
    earlier = jnp.dot(before.astype(BF), hits.astype(BF), preferred_element_type=F32)
    placed = jnp.logical_and(source == row // share, earlier == slot.astype(F32))
    table = jnp.where(placed, hits, 0.0)
    if gates:
        mixing = table * gate
        high = mixing.astype(BF)
        table_ref[: ZH * share, :] = high
        table_ref[ZH * share :, :] = (mixing - high.astype(F32)).astype(BF)
    else:
        table_ref[...] = table.T.astype(BF)


def slot_table(where, ring, gates):
    slots = Y * X * ZL * ZH * CAP
    count = ZH * (ring.shape[1] - HEAD)
    vmem = pl.BlockSpec(memory_space=pltpu.VMEM)
    return pl.pallas_call(
        functools.partial(table_kernel, gates),
        out_shape=jax.ShapeDtypeStruct((2 * count, slots) if gates else (slots, count), BF),
        in_specs=[pl.BlockSpec(memory_space=pltpu.SMEM), vmem],
        out_specs=vmem,
        cost_estimate=pl.CostEstimate(flops=3000000, bytes_accessed=400000, transcendentals=0),
        name="gates" if gates else "table",
    )(where, ring)


def route_kernel(table_ref, *refs):
    rows, out_ref = refs[:-1], refs[-1]
    whole = jnp.concatenate([ref[...] for ref in rows], axis=0)
    for i in range(D // SPAN):
        part = slice(i * SPAN, (i + 1) * SPAN)
        out_ref[:, part] = jnp.dot(
            table_ref[...], whole[:, part], preferred_element_type=F32
        ).astype(BF)


def route(table, rows):
    vmem = pl.BlockSpec(memory_space=pltpu.VMEM)
    return pl.pallas_call(
        route_kernel,
        out_shape=jax.ShapeDtypeStruct((table.shape[0], D), BF),
        in_specs=[vmem] * (1 + len(rows)),
        out_specs=vmem,
        cost_estimate=pl.CostEstimate(flops=70000000, bytes_accessed=1400000, transcendentals=0),
        name="route",
    )(table, *rows)


def expert_kernel(rows_ref, *refs):
    pieces = refs[:8]
    out_ref, weights, active, out, sems, out_sems = refs[8:]
    width = pieces[0].shape[0] // 3

    def fetch(part, i):
        return pltpu.make_async_copy(
            pieces[i].at[pl.ds(part * width, width)],
            weights.at[part, pl.ds(i * width, width)],
            sems.at[part, i],
        )

    for half in range(2):
        for part in range(2):
            for i in range(4):
                fetch(part, 4 * half + i).start()
    for i in range(8):
        fetch(2, i).start()
    rows = rows_ref[...]
    for half in range(2):
        for part in range(2):
            for i in range(4):
                fetch(part, 4 * half + i).wait()
        span = slice(4 * half * width, 4 * (half + 1) * width)
        gate = lax.dot_general(
            weights[0, span], rows, (((1,), (1,)), ((), ())), preferred_element_type=F32
        )
        up = lax.dot_general(
            weights[1, span], rows, (((1,), (1,)), ((), ())), preferred_element_type=F32
        )
        active[span, :] = (gate / (1.0 + jnp.exp(-gate)) * up).astype(BF)
    for i in range(8):
        fetch(2, i).wait()
    acts = active[...].T
    copies = []
    for i in range(D // SPAN):
        out[i] = jnp.dot(
            acts, weights[2, :, i * SPAN : (i + 1) * SPAN], preferred_element_type=F32
        ).astype(BF)
        copies.append(
            pltpu.make_async_copy(out.at[i], out_ref.at[:, pl.ds(i * SPAN, SPAN)], out_sems.at[i])
        )
        copies[i].start()
    for copy in copies:
        copy.wait()


def expert(rows, pieces):
    count = rows.shape[0]
    width = pieces[0].shape[0] // 3
    vmem = pl.BlockSpec(memory_space=pltpu.VMEM)
    hbm = pl.BlockSpec(memory_space=pl.ANY)
    return pl.pallas_call(
        expert_kernel,
        out_shape=jax.ShapeDtypeStruct((count, D), BF),
        in_specs=[vmem] + [hbm] * 8,
        out_specs=pl.BlockSpec(memory_space=pltpu.HBM),
        scratch_shapes=[
            pltpu.VMEM((3, 8 * width, D), BF),
            pltpu.VMEM((8 * width, count), BF),
            pltpu.VMEM((D // SPAN, count, SPAN), BF),
            pltpu.SemaphoreType.DMA((3, 8)),
            pltpu.SemaphoreType.DMA((D // SPAN,)),
        ],
        compiler_params=pltpu.CompilerParams(vmem_limit_bytes=EXPERT_VMEM),
        cost_estimate=pl.CostEstimate(
            flops=2400000000, bytes_accessed=11500000, transcendentals=200000
        ),
        name="expert",
    )(rows, *pieces)


def pack_kernel(x_ref, gate_ref, up_ref, down_ref, *refs):
    outs, sems = refs[:X], refs[X]
    width = down_ref.shape[1]

    def copy(k, part):
        source = (gate_ref, up_ref, down_ref)[part]
        return pltpu.make_async_copy(
            source.at[(x_ref[0] + k) % X],
            outs[k].at[pl.ds(part * width, width)],
            sems.at[k, part],
        )

    for k in range(X):
        for part in range(3):
            copy(k, part).start()
    for k in range(X):
        for part in range(3):
            copy(k, part).wait()


def pack(x, gate_t, up_t, w_down):
    width = w_down.shape[1]
    hbm = pl.BlockSpec(memory_space=pl.ANY)
    return pl.pallas_call(
        pack_kernel,
        out_shape=[jax.ShapeDtypeStruct((3 * width, D), BF)] * X,
        in_specs=[pl.BlockSpec(memory_space=pltpu.SMEM), hbm, hbm, hbm],
        out_specs=[pl.BlockSpec(memory_space=pltpu.VMEM)] * X,
        scratch_shapes=[pltpu.SemaphoreType.DMA((X, 3))],
        cost_estimate=pl.CostEstimate(flops=0, bytes_accessed=9500000, transcendentals=0),
        name="pack",
    )(x.reshape(1).astype(jnp.int32), gate_t, up_t, w_down)


def spread(piece, axes, members):
    copies = jnp.broadcast_to(piece[None], (members, *piece.shape))
    return lax.all_to_all(copies, axes, 0, 0, tiled=True)


def turned(axis_size, by):
    return [(i, (i + by) % axis_size) for i in range(axis_size)]


def weight_pieces(w_gate, w_up, w_down, c, x, zl):
    packed = pack(x, jnp.swapaxes(w_gate, 1, 2), jnp.swapaxes(w_up, 1, 2), w_down)

    def shifted(k, straight, crossing):
        return [
            ((cs * X + xs) * ZL + zs, (zs * X + (xs + k) % X) * ZL + cs)
            for cs in range(C)
            for xs in range(X)
            for zs in range(ZL)
            if (straight if cs == zs else crossing)
        ]

    axes = ("c", "x", "zl")
    own = []
    for k in range(X):
        if k in SPLIT:
            straight = lax.ppermute(packed[k], axes, shifted(k, True, False))
            moved = lax.ppermute(packed[k], axes, shifted(k, False, True))
        else:
            straight = packed[k]
            moved = lax.ppermute(packed[k], axes, shifted(k, k > 0, True))
        if k == 0 or k in SPLIT:
            moved = jnp.where(zl == c, straight, moved)
        own.append(moved)
    other = []
    for k in range(X):
        other.append(lax.ppermute(own[k], "c", [(0, 1), (1, 0)]))
    return own + other


def on_device(
    tokens,
    attn_gain,
    w_query,
    w_key,
    w_value,
    query_gain,
    key_gain,
    w_out,
    moe_gain,
    expert_ids,
    expert_weights,
    w_gate,
    w_up,
    w_down,
):
    zh, y, c = lax.axis_index("zh"), lax.axis_index("y"), lax.axis_index("c")
    x, zl = lax.axis_index("x"), lax.axis_index("zl")
    sec = (zh * Y + y) * C + c
    narrow = x * ZL + zl
    local_rows = tokens.shape[0]
    share = local_rows // (X * ZL)
    positions = sec * local_rows + jnp.arange(local_rows, dtype=jnp.int32)
    cosine, sine = angles_of(positions)
    half = HEAD // 2

    pieces = weight_pieces(w_gate, w_up, w_down, c, x, zl)

    normed = rms_norm(tokens, attn_gain).astype(BF)

    def columns(w):
        turned_w = lax.dot_general(
            w, normed, (((0,), (1,)), ((), ())), preferred_element_type=F32
        )
        return jnp.swapaxes(turned_w.reshape(-1, KV_HEADS, local_rows), 0, 1)

    both = jnp.stack([columns(w_key), columns(w_value)], axis=1)
    both = both.reshape(X * ZL, -1, local_rows)
    one = lax.all_to_all(both, NARROW, 0, 0, tiled=True).reshape(HEAD, local_rows)
    key_t = one * lax.rsqrt(jnp.mean(one * one, axis=0, keepdims=True) + norm_eps)
    key_t = key_t * key_gain[:, None]
    cos_t, sin_t = cosine.T, sine.T
    lead, trail = key_t[:half], key_t[half:]
    key_t = jnp.concatenate(
        [lead * cos_t - trail * sin_t, trail * cos_t + lead * sin_t], axis=0
    ).astype(BF)
    piece = jnp.where(zl == 0, key_t, one.T.astype(BF))

    ids = lax.dynamic_slice_in_dim(expert_ids, narrow * share, share, 0)
    weights = lax.dynamic_slice_in_dim(expert_weights, narrow * share, share, 0)
    gates = weights / jnp.sum(weights, axis=-1, keepdims=True)
    gates_high = gates.astype(BF)
    gates_low = (gates - gates_high.astype(F32)).astype(BF)
    tail = jnp.concatenate(
        [ids.astype(BF), gates_high, gates_low, jnp.zeros((share, HEAD - 3 * TOPK), BF)], axis=1
    )
    ring = spread(jnp.concatenate([piece, tail], axis=0), ("zh", "zl"), ZH * ZL)
    own = spread(ring[:, :HEAD], "y", Y)
    own = own.reshape(Y, ZH, ZL, HEAD, HEAD)
    other = lax.ppermute(own, "c", [(0, 1), (1, 0)])

    query = jnp.dot(normed, w_query, preferred_element_type=F32)
    where = jnp.stack([zh * Y + y, c]).astype(jnp.int32)
    place = jnp.stack([zh, zl]).astype(jnp.int32)
    cosines = jnp.concatenate([cosine, cosine], axis=1)
    sines = jnp.concatenate([-sine, sine], axis=1)
    partial = attention(
        where, query, cosines, sines, query_gain.reshape(1, -1), own, other, w_out
    )
    partial, tokens = lax.optimization_barrier((partial, tokens))
    blocks = lax.all_to_all(partial.reshape(X * ZL, share, D), NARROW, 0, 0, tiled=True)
    own_tokens = lax.dynamic_slice_in_dim(tokens, narrow * share, share, 0)
    carried, moe_in = carry(blocks, own_tokens, moe_gain)

    rows = [moe_in] + [lax.ppermute(moe_in, "zh", turned(ZH, k)) for k in range(1, ZH)]
    table = slot_table(place, ring, False)
    outgoing = route(table, rows)
    arrived = lax.all_to_all(
        outgoing.reshape(Y * X * ZL, ZH * CAP, D), PLANE, 0, 0, tiled=True
    ).reshape(-1, D)
    answers = expert(arrived, pieces)
    returned = lax.all_to_all(
        answers.reshape(Y * X * ZL, ZH * CAP, D), PLANE, 0, 0, tiled=True
    ).reshape(-1, D)
    mixing = slot_table(place, ring, True)
    sums = jnp.dot(mixing, returned, preferred_element_type=F32)
    sums = sums[: ZH * share] + sums[ZH * share :]
    sums = sums.reshape(ZH, share, D)
    result = carried.astype(F32) + sums[0]
    for k in range(1, ZH):
        back = lax.ppermute(sums[k].astype(BF), "zh", turned(ZH, -k))
        result = result + back.astype(F32)
    return result.astype(BF)


def solution(mesh):
    split = Mesh(mesh.devices.reshape(ZH, Y, C, X, ZL), ("zh", "y", "c", "x", "zl"))
    in_specs = (
        P(SEC, None),
        P(),
        P(None, NARROW),
        P(None, NARROW),
        P(None, NARROW),
        P(),
        P(),
        P(NARROW, None),
        P(),
        P(SEC, None),
        P(SEC, None),
        P(SEC, None, NARROW),
        P(SEC, None, NARROW),
        P(SEC, NARROW, None),
    )
    out_specs = P(SEC + NARROW, None)

    return jax.shard_map(
        on_device, mesh=split, in_specs=in_specs, out_specs=out_specs, check_vma=False
    )
```

```python
import functools
import math

import jax
import jax.numpy as jnp
from jax import lax
from jax.experimental import pallas as pl
from jax.experimental.pallas import tpu as pltpu
from jax.sharding import Mesh
from jax.sharding import PartitionSpec as P


D = 2048
KV_HEADS = 4
HEAD = 128
TOPK = 8
CAP = 2
SPAN = 512
ZH, Y, C, X, ZL = 4, 4, 2, 4, 2
SEC = ("zh", "y", "c")
NARROW = ("x", "zl")
PLANE = ("y", "x", "zl")

norm_eps = 1e-06
SPLIT = (2,)
EXPERT_VMEM = 60 * 1024 * 1024
BF = jnp.bfloat16
F32 = jnp.float32


def rms_norm(inputs, gain):
    widened = inputs.astype(F32)
    return (
        widened * lax.rsqrt(jnp.mean(widened * widened, axis=-1, keepdims=True) + norm_eps) * gain
    )


def angles_of(positions):
    half = HEAD // 2
    inverse = jnp.exp(-jnp.log(1000000.0) * jnp.arange(half, dtype=F32) * 2.0 / HEAD)
    angles = positions.astype(F32)[:, None] * inverse[None, :]
    return jnp.cos(angles), jnp.sin(angles)


def attention_kernel(
    where_ref, q_ref, cos_ref, sin_ref, gain_ref, own_ref, other_ref, w_out_ref, out_ref, q_all, acc, peak, total, attended, w_out, sem
):
    rows = q_ref.shape[0]
    heads = q_ref.shape[1] // HEAD
    pair_here, core = where_ref[0], where_ref[1]
    factor = math.log2(math.e) / math.sqrt(HEAD)
    fetch = pltpu.make_async_copy(w_out_ref, w_out, sem)
    fetch.start()
    for h in range(heads):
        q = q_ref[:, h * HEAD : (h + 1) * HEAD]
        q = q * lax.rsqrt(jnp.mean(q * q, axis=-1, keepdims=True) + norm_eps) * gain_ref[...]
        q = q * cos_ref[...] + pltpu.roll(q, HEAD // 2, 1) * sin_ref[...]
        q_all[h * rows : (h + 1) * rows, :] = q.astype(BF)
    acc[...] = jnp.zeros_like(acc)
    total[...] = jnp.zeros_like(total)
    peak[...] = jnp.full_like(peak, -1e30)

    def step(group, last):
        zh = group // 2
        y = group % 2 * 2
        sources = ((own_ref, y), (other_ref, y), (own_ref, y + 1), (other_ref, y + 1))
        keys = jnp.concatenate([ref[at, zh, 0] for ref, at in sources], axis=1)
        values = jnp.concatenate([ref[at, zh, 1] for ref, at in sources], axis=0)
        s = jnp.dot(q_all[...], keys, preferred_element_type=F32)
        if last:
            row = lax.broadcasted_iota(jnp.int32, s.shape, 0) % rows
            column = lax.broadcasted_iota(jnp.int32, s.shape, 1)
            piece = column // HEAD
            section = 4 * group + piece // 2 * 2 + jnp.where(piece % 2 == 0, core, 1 - core)
            allowed = section * HEAD + column % HEAD <= (2 * pair_here + core) * rows + row
            s = jnp.where(allowed, s, -1e30)
        parts = [s[:, i * HEAD : (i + 1) * HEAD] for i in range(4)]
        highest = jnp.maximum(jnp.maximum(parts[0], parts[1]), jnp.maximum(parts[2], parts[3]))
        old = peak[...]
        new = jnp.maximum(old, jnp.max(highest, axis=-1, keepdims=True))
        p = jnp.exp2((s - new) * factor)
        if last:
            p = jnp.where(allowed, p, 0.0)
        parts = [p[:, i * HEAD : (i + 1) * HEAD] for i in range(4)]
        scale = jnp.exp2((old - new) * factor)
        total[...] = total[...] * scale + ((parts[0] + parts[1]) + (parts[2] + parts[3]))
        acc[...] = acc[...] * scale + jnp.dot(p.astype(BF), values, preferred_element_type=F32)
        peak[...] = new

    @pl.loop(0, pair_here // 2)
    def _(group):
        step(group, False)

    step(pair_here // 2, True)
    summed = jnp.sum(total[...], axis=-1, keepdims=True)
    for h in range(heads):
        part = slice(h * rows, (h + 1) * rows)
        attended[:, h * HEAD : (h + 1) * HEAD] = (acc[part, :] / summed[part]).astype(BF)
    fetch.wait()
    for i in range(D // SPAN):
        part = slice(i * SPAN, (i + 1) * SPAN)
        out_ref[:, part] = jnp.dot(
            attended[...], w_out[:, part], preferred_element_type=F32
        ).astype(BF)


def attention(where, query, cosine, sine, gain, own, other, w_out):
    rows = query.shape[0]
    heads = query.shape[1] // HEAD
    vmem = pl.BlockSpec(memory_space=pltpu.VMEM)
    return pl.pallas_call(
        attention_kernel,
        out_shape=jax.ShapeDtypeStruct((rows, D), BF),
        in_specs=[pl.BlockSpec(memory_space=pltpu.SMEM)]
        + [vmem] * 6
        + [pl.BlockSpec(memory_space=pl.ANY)],
        out_specs=vmem,
        scratch_shapes=[
            pltpu.VMEM((heads * rows, HEAD), BF),
            pltpu.VMEM((heads * rows, HEAD), F32),
            pltpu.VMEM((heads * rows, 1), F32),
            pltpu.VMEM((heads * rows, HEAD), F32),
            pltpu.VMEM((rows, heads * HEAD), BF),
            pltpu.VMEM(w_out.shape, BF),
            pltpu.SemaphoreType.DMA,
        ],
        cost_estimate=pl.CostEstimate(
            flops=1400000000, bytes_accessed=5000000, transcendentals=2000000
        ),
        name="attend",
    )(where, query, cosine, sine, gain, own, other, w_out)


def carry_kernel(blocks_ref, tokens_ref, gain_ref, carried_ref, normed_ref):
    mixed = jnp.sum(blocks_ref[...].astype(F32), axis=0)
    carried = (tokens_ref[...].astype(F32) + mixed).astype(BF)
    carried_ref[...] = carried
    normed_ref[...] = rms_norm(carried, gain_ref[...]).astype(BF)


def carry(blocks, tokens, gain):
    vmem = pl.BlockSpec(memory_space=pltpu.VMEM)
    shape = jax.ShapeDtypeStruct(tokens.shape, BF)
    return pl.pallas_call(
        carry_kernel,
        out_shape=[shape, shape],
        in_specs=[vmem] * 3,
        out_specs=[vmem] * 2,
        cost_estimate=pl.CostEstimate(flops=600000, bytes_accessed=800000, transcendentals=16),
        name="carry",
    )(blocks, tokens, gain.reshape(1, -1))


def table_kernel(gates, where_ref, ring_ref, table_ref):
    zh, zl = where_ref[0], where_ref[1]
    share = ring_ref.shape[1] - HEAD
    tails = jnp.concatenate(
        [ring_ref[(zh + ZH - k) % ZH * ZL + zl, HEAD:, :] for k in range(ZH)], axis=0
    ).astype(F32)
    shape = (ZH * share, Y * X * ZL * ZH * CAP)
    row = lax.broadcasted_iota(jnp.int32, shape, 0)
    column = lax.broadcasted_iota(jnp.int32, shape, 1)
    slot, source, chip = column % CAP, column // CAP % ZH, column // (CAP * ZH)
    expert_of = (
        zh * (Y * X * ZL) + chip // (X * ZL) * (X * ZL) + chip % ZL * X + chip // ZL % X
    ).astype(F32)
    hits = jnp.zeros(shape, F32)
    gate = jnp.zeros(shape, F32)
    for k in range(TOPK):
        same = tails[:, k : k + 1] == expert_of
        weight = tails[:, TOPK + k : TOPK + k + 1] + tails[:, 2 * TOPK + k : 2 * TOPK + k + 1]
        hits = jnp.where(same, 1.0, hits)
        gate = jnp.where(same, weight, gate)
    one = lax.broadcasted_iota(jnp.int32, (ZH * share, ZH * share), 0)
    two = lax.broadcasted_iota(jnp.int32, (ZH * share, ZH * share), 1)
    before = jnp.where(jnp.logical_and(two < one, two // share == one // share), 1.0, 0.0)
    earlier = jnp.dot(before.astype(BF), hits.astype(BF), preferred_element_type=F32)
    placed = jnp.logical_and(source == row // share, earlier == slot.astype(F32))
    table = jnp.where(placed, hits, 0.0)
    if gates:
        mixing = table * gate
        high = mixing.astype(BF)
        table_ref[: ZH * share, :] = high
        table_ref[ZH * share :, :] = (mixing - high.astype(F32)).astype(BF)
    else:
        table_ref[...] = table.T.astype(BF)


def slot_table(where, ring, gates):
    slots = Y * X * ZL * ZH * CAP
    count = ZH * (ring.shape[1] - HEAD)
    vmem = pl.BlockSpec(memory_space=pltpu.VMEM)
    return pl.pallas_call(
        functools.partial(table_kernel, gates),
        out_shape=jax.ShapeDtypeStruct((2 * count, slots) if gates else (slots, count), BF),
        in_specs=[pl.BlockSpec(memory_space=pltpu.SMEM), vmem],
        out_specs=vmem,
        cost_estimate=pl.CostEstimate(flops=3000000, bytes_accessed=400000, transcendentals=0),
        name="gates" if gates else "table",
    )(where, ring)


def route_kernel(table_ref, *refs):
    rows, out_ref = refs[:-1], refs[-1]
    whole = jnp.concatenate([ref[...] for ref in rows], axis=0)
    for i in range(D // SPAN):
        part = slice(i * SPAN, (i + 1) * SPAN)
        out_ref[:, part] = jnp.dot(
            table_ref[...], whole[:, part], preferred_element_type=F32
        ).astype(BF)


def route(table, rows):
    vmem = pl.BlockSpec(memory_space=pltpu.VMEM)
    return pl.pallas_call(
        route_kernel,
        out_shape=jax.ShapeDtypeStruct((table.shape[0], D), BF),
        in_specs=[vmem] * (1 + len(rows)),
        out_specs=vmem,
        cost_estimate=pl.CostEstimate(flops=70000000, bytes_accessed=1400000, transcendentals=0),
        name="route",
    )(table, *rows)


def expert_kernel(rows_ref, *refs):
    pieces = refs[:8]
    out_ref, weights, active, out, sems, out_sems = refs[8:]
    width = pieces[0].shape[0] // 3

    def fetch(part, i):
        return pltpu.make_async_copy(
            pieces[i].at[pl.ds(part * width, width)],
            weights.at[part, pl.ds(i * width, width)],
            sems.at[part, i],
        )

    for half in range(2):
        for part in range(2):
            for i in range(4):
                fetch(part, 4 * half + i).start()
    for i in range(8):
        fetch(2, i).start()
    rows = rows_ref[...]
    for half in range(2):
        for part in range(2):
            for i in range(4):
                fetch(part, 4 * half + i).wait()
        span = slice(4 * half * width, 4 * (half + 1) * width)
        gate = lax.dot_general(
            weights[0, span], rows, (((1,), (1,)), ((), ())), preferred_element_type=F32
        )
        up = lax.dot_general(
            weights[1, span], rows, (((1,), (1,)), ((), ())), preferred_element_type=F32
        )
        active[span, :] = (gate / (1.0 + jnp.exp(-gate)) * up).astype(BF)
    for i in range(8):
        fetch(2, i).wait()
    acts = active[...].T
    copies = []
    for i in range(D // SPAN):
        out[i] = jnp.dot(
            acts, weights[2, :, i * SPAN : (i + 1) * SPAN], preferred_element_type=F32
        ).astype(BF)
        copies.append(
            pltpu.make_async_copy(out.at[i], out_ref.at[:, pl.ds(i * SPAN, SPAN)], out_sems.at[i])
        )
        copies[i].start()
    for copy in copies:
        copy.wait()


def expert(rows, pieces):
    count = rows.shape[0]
    width = pieces[0].shape[0] // 3
    vmem = pl.BlockSpec(memory_space=pltpu.VMEM)
    hbm = pl.BlockSpec(memory_space=pl.ANY)
    return pl.pallas_call(
        expert_kernel,
        out_shape=jax.ShapeDtypeStruct((count, D), BF),
        in_specs=[vmem] + [hbm] * 8,
        out_specs=pl.BlockSpec(memory_space=pltpu.HBM),
        scratch_shapes=[
            pltpu.VMEM((3, 8 * width, D), BF),
            pltpu.VMEM((8 * width, count), BF),
            pltpu.VMEM((D // SPAN, count, SPAN), BF),
            pltpu.SemaphoreType.DMA((3, 8)),
            pltpu.SemaphoreType.DMA((D // SPAN,)),
        ],
        compiler_params=pltpu.CompilerParams(vmem_limit_bytes=EXPERT_VMEM),
        cost_estimate=pl.CostEstimate(
            flops=2400000000, bytes_accessed=11500000, transcendentals=200000
        ),
        name="expert",
    )(rows, *pieces)


def pack_kernel(x_ref, gate_ref, up_ref, down_ref, *refs):
    outs, held, sems, out_sems = refs[:X], refs[X], refs[X + 1], refs[X + 2]
    width = down_ref.shape[1]

    def fetch(k, part):
        source = (gate_ref, up_ref, down_ref)[part]
        return pltpu.make_async_copy(
            source.at[(x_ref[0] + k) % X],
            held.at[k, pl.ds(part * width, width)],
            sems.at[k, part],
        )

    def store(k):
        return pltpu.make_async_copy(held.at[k], outs[k], out_sems.at[k])

    for k in range(X):
        for part in range(3):
            fetch(k, part).start()
    for k in range(X):
        for part in range(3):
            fetch(k, part).wait()
        store(k).start()
    for k in range(X):
        store(k).wait()


def pack(x, gate_t, up_t, w_down):
    width = w_down.shape[1]
    hbm = pl.BlockSpec(memory_space=pl.ANY)
    return pl.pallas_call(
        pack_kernel,
        out_shape=[jax.ShapeDtypeStruct((3 * width, D), BF)] * X,
        in_specs=[pl.BlockSpec(memory_space=pltpu.SMEM), hbm, hbm, hbm],
        out_specs=[hbm] * X,
        scratch_shapes=[
            pltpu.VMEM((X, 3 * width, D), BF),
            pltpu.SemaphoreType.DMA((X, 3)),
            pltpu.SemaphoreType.DMA((X,)),
        ],
        cost_estimate=pl.CostEstimate(flops=0, bytes_accessed=9500000, transcendentals=0),
        name="pack",
    )(x.reshape(1).astype(jnp.int32), gate_t, up_t, w_down)


def columns_kernel(tokens_ref, gain_ref, key_ref, value_ref, normed_ref, out_ref, held):
    normed = rms_norm(tokens_ref[...], gain_ref[...]).astype(BF)
    normed_ref[...] = normed
    entries = out_ref.shape[1]
    for i, ref in enumerate((key_ref, value_ref)):
        held[i] = lax.dot_general(
            ref[...], normed, (((1,), (1,)), ((), ())), preferred_element_type=F32
        )
        for h in range(KV_HEADS):
            out_ref[2 * h + i] = held[i, pl.ds(h, entries, stride=KV_HEADS), :]


def columns(tokens, gain, key_t, value_t):
    rows = tokens.shape[0]
    width = key_t.shape[0]
    vmem = pl.BlockSpec(memory_space=pltpu.VMEM)
    return pl.pallas_call(
        columns_kernel,
        out_shape=[
            jax.ShapeDtypeStruct(tokens.shape, BF),
            jax.ShapeDtypeStruct((2 * KV_HEADS, width // KV_HEADS, rows), F32),
        ],
        in_specs=[vmem] * 4,
        out_specs=[vmem] * 2,
        scratch_shapes=[pltpu.VMEM((2, width, rows), F32)],
        cost_estimate=pl.CostEstimate(flops=70000000, bytes_accessed=1700000, transcendentals=128),
        name="columns",
    )(tokens, gain.reshape(1, -1), key_t, value_t)


def spread(piece, axes, members):
    copies = jnp.broadcast_to(piece[None], (members, *piece.shape))
    return lax.all_to_all(copies, axes, 0, 0, tiled=True)


def turned(axis_size, by):
    return [(i, (i + by) % axis_size) for i in range(axis_size)]


def weight_pieces(w_gate, w_up, w_down, c, x, zl):
    packed = pack(x, jnp.swapaxes(w_gate, 1, 2), jnp.swapaxes(w_up, 1, 2), w_down)

    def shifted(k, straight, crossing):
        return [
            ((cs * X + xs) * ZL + zs, (zs * X + (xs + k) % X) * ZL + cs)
            for cs in range(C)
            for xs in range(X)
            for zs in range(ZL)
            if (straight if cs == zs else crossing)
        ]

    axes = ("c", "x", "zl")
    own = []
    for k in range(X):
        if k in SPLIT:
            straight = lax.ppermute(packed[k], axes, shifted(k, True, False))
            moved = lax.ppermute(packed[k], axes, shifted(k, False, True))
        else:
            straight = packed[k]
            moved = lax.ppermute(packed[k], axes, shifted(k, k > 0, True))
        if k == 0 or k in SPLIT:
            moved = jnp.where(zl == c, straight, moved)
        own.append(moved)
    other = []
    for k in range(X):
        other.append(lax.ppermute(own[k], "c", [(0, 1), (1, 0)]))
    return own + other


def on_device(
    tokens,
    attn_gain,
    w_query,
    w_key,
    w_value,
    query_gain,
    key_gain,
    w_out,
    moe_gain,
    expert_ids,
    expert_weights,
    w_gate,
    w_up,
    w_down,
):
    zh, y, c = lax.axis_index("zh"), lax.axis_index("y"), lax.axis_index("c")
    x, zl = lax.axis_index("x"), lax.axis_index("zl")
    sec = (zh * Y + y) * C + c
    narrow = x * ZL + zl
    local_rows = tokens.shape[0]
    share = local_rows // (X * ZL)
    positions = sec * local_rows + jnp.arange(local_rows, dtype=jnp.int32)
    cosine, sine = angles_of(positions)
    half = HEAD // 2

    pieces = weight_pieces(w_gate, w_up, w_down, c, x, zl)

    normed, both = columns(tokens, attn_gain, w_key.T, w_value.T)
    one = lax.all_to_all(both, NARROW, 0, 0, tiled=True).reshape(HEAD, local_rows)
    key_t = one * lax.rsqrt(jnp.mean(one * one, axis=0, keepdims=True) + norm_eps)
    key_t = key_t * key_gain[:, None]
    cos_t, sin_t = cosine.T, sine.T
    lead, trail = key_t[:half], key_t[half:]
    key_t = jnp.concatenate(
        [lead * cos_t - trail * sin_t, trail * cos_t + lead * sin_t], axis=0
    ).astype(BF)
    piece = jnp.where(zl == 0, key_t, one.T.astype(BF))

    ids = lax.dynamic_slice_in_dim(expert_ids, narrow * share, share, 0)
    weights = lax.dynamic_slice_in_dim(expert_weights, narrow * share, share, 0)
    gates = weights / jnp.sum(weights, axis=-1, keepdims=True)
    gates_high = gates.astype(BF)
    gates_low = (gates - gates_high.astype(F32)).astype(BF)
    tail = jnp.concatenate(
        [ids.astype(BF), gates_high, gates_low, jnp.zeros((share, HEAD - 3 * TOPK), BF)], axis=1
    )
    ring = spread(jnp.concatenate([piece, tail], axis=0), ("zh", "zl"), ZH * ZL)
    own = spread(ring[:, :HEAD], "y", Y)
    own = own.reshape(Y, ZH, ZL, HEAD, HEAD)
    other = lax.ppermute(own, "c", [(0, 1), (1, 0)])

    query = jnp.dot(normed, w_query, preferred_element_type=F32)
    where = jnp.stack([zh * Y + y, c]).astype(jnp.int32)
    place = jnp.stack([zh, zl]).astype(jnp.int32)
    cosines = jnp.concatenate([cosine, cosine], axis=1)
    sines = jnp.concatenate([-sine, sine], axis=1)
    partial = attention(
        where, query, cosines, sines, query_gain.reshape(1, -1), own, other, w_out
    )
    partial, tokens = lax.optimization_barrier((partial, tokens))
    blocks = lax.all_to_all(partial.reshape(X * ZL, share, D), NARROW, 0, 0, tiled=True)
    own_tokens = lax.dynamic_slice_in_dim(tokens, narrow * share, share, 0)
    carried, moe_in = carry(blocks, own_tokens, moe_gain)

    rows = [moe_in] + [lax.ppermute(moe_in, "zh", turned(ZH, k)) for k in range(1, ZH)]
    table = slot_table(place, ring, False)
    outgoing = route(table, rows)
    arrived = lax.all_to_all(
        outgoing.reshape(Y * X * ZL, ZH * CAP, D), PLANE, 0, 0, tiled=True
    ).reshape(-1, D)
    answers = expert(arrived, pieces)
    returned = lax.all_to_all(
        answers.reshape(Y * X * ZL, ZH * CAP, D), PLANE, 0, 0, tiled=True
    ).reshape(-1, D)
    mixing = slot_table(place, ring, True)
    sums = jnp.dot(mixing, returned, preferred_element_type=F32)
    sums = sums[: ZH * share] + sums[ZH * share :]
    sums = sums.reshape(ZH, share, D)
    result = carried.astype(F32) + sums[0]
    for k in range(1, ZH):
        back = lax.ppermute(sums[k].astype(BF), "zh", turned(ZH, -k))
        result = result + back.astype(F32)
    return result.astype(BF)


def solution(mesh):
    split = Mesh(mesh.devices.reshape(ZH, Y, C, X, ZL), ("zh", "y", "c", "x", "zl"))
    in_specs = (
        P(SEC, None),
        P(),
        P(None, NARROW),
        P(None, NARROW),
        P(None, NARROW),
        P(),
        P(),
        P(NARROW, None),
        P(),
        P(SEC, None),
        P(SEC, None),
        P(SEC, None, NARROW),
        P(SEC, None, NARROW),
        P(SEC, NARROW, None),
    )
    out_specs = P(SEC + NARROW, None)

    return jax.shard_map(
        on_device, mesh=split, in_specs=in_specs, out_specs=out_specs, check_vma=False
    )
```
